512 devices in a mesh: ply: 16 (over z_hi, y), tile: 32 (over z_lo, x, core).
Axes of the slice: x: 4, y: 8, z: 8 (z_hi: 2, z_lo: 4; z = z_hi * 4 + z_lo), core: 2. Of those that a mesh axis runs over, the one named last changes fastest.
Arguments:
- scaled_warmth: float32 [64, 256, 1024], P('ply', 'tile'), may hold values from 0.9 to 1.1
- crosslink_fraction: float32 [64, 256, 1024], P('ply', 'tile'), may hold values from 0 to 0.4
- fluid_stress: float32 [64, 256, 1024], P('ply', 'tile'), may hold values from 0 to 1
- preform_porosity_coefficient: float32 [64, 256, 1024], P('ply', 'tile'), may hold values from 0.02 to 0.2
- wetted_flags: int32 [64, 256, 1024], P('ply', 'tile'), may hold values 0 or 1
- injection_flags: int32 [64, 256, 1024], P('ply', 'tile'), may hold values 0 or 1
- outlet_flags: int32 [64, 256, 1024], P('ply', 'tile'), may hold values 0 or 1
Outputs:
- temperature_out: float32 [64, 256, 1024], P('ply', 'tile')
- cure_out: float32 [64, 256, 1024], P('ply', 'tile')
- pressure_out: float32 [64, 256, 1024], P('ply', 'tile')
- imbalance_record: float32 [2], replicated
The draws below stay inside these ranges and needn't reach their ends.
All inputs are finite; a program needn't handle non-finite values. No bound on the sum of `wetted_flags` or of `injection_flags` or of `outlet_flags` on one device may be relied on, other than what follows from the above.
Results may differ from the reference program's by a relative error of at most 0.0003.
Values sent between devices are 32-bit elements; how exact they have to be, the bound alone decides.
No kernel may reach another device: no remote copies, remote signals or barrier semaphores. Data moves between devices by JAX's collectives and lax.ppermute only.
A program may use at most 64 MiB of HBM per device.

```python
import math
import jax
import jax.numpy as jnp

GRID_CROSSWISE = 1024
STEPS = 2
SWEEPS = 4
LAMINA_TOTAL = 64
GRID_LENGTHWISE = 256


def plant(entries, rng, smallest, high):
    dims = entries.shape
    spot = [jax.random.randint(jax.random.fold_in(rng, axis), (), 0, dims[axis]) for axis in range(len(dims))]
    entries = entries.at[tuple(spot)].set(smallest)
    longest = dims.index(max(dims))
    spot[longest] = (spot[longest] + 1) % dims[longest]
    return entries.at[tuple(spot)].set(high)


def levels(key, dims, pieces, least, top_value):
    gain = 1.0
    for dim, shards_of in pieces:
        steps = jax.random.uniform(jax.random.fold_in(jax.random.fold_in(key, 6), dim), (shards_of,), jnp.float32, least / len(pieces), top_value / len(pieces))
        gain = gain * jnp.repeat(jnp.exp(steps), dims[dim] // shards_of).reshape((-1,) + (1,) * (len(dims) - 1 - dim))
    return gain


def setup_inputs(seed: int = 0) -> dict:
    arg_keys = jax.random.split(jax.random.key(seed), 8)
    scaled_warmth = jnp.clip(0.9 + 0.20000005 * jax.random.uniform(arg_keys[0], (LAMINA_TOTAL, GRID_LENGTHWISE, GRID_CROSSWISE), jnp.float32) ** levels(arg_keys[0], (LAMINA_TOTAL, GRID_LENGTHWISE, GRID_CROSSWISE), ((0, 16), (1, 32)), -0.2, 0.2), 0.9, 1.1)
    crosslink_fraction = jnp.clip(0.4 * jax.random.uniform(arg_keys[1], (LAMINA_TOTAL, GRID_LENGTHWISE, GRID_CROSSWISE), jnp.float32) ** levels(arg_keys[1], (LAMINA_TOTAL, GRID_LENGTHWISE, GRID_CROSSWISE), ((0, 16), (1, 32)), -0.2, 0.2), 0.0, 0.4)
    fluid_stress = jnp.clip(1.0 * jax.random.uniform(arg_keys[2], (LAMINA_TOTAL, GRID_LENGTHWISE, GRID_CROSSWISE), jnp.float32) ** levels(arg_keys[2], (LAMINA_TOTAL, GRID_LENGTHWISE, GRID_CROSSWISE), ((0, 16), (1, 32)), -0.2, 0.2), 0.0, 1.0)
    preform_porosity_coefficient = jnp.clip(jnp.exp(math.log(0.2) - 2.3025851 * jax.random.uniform(arg_keys[3], (LAMINA_TOTAL, GRID_LENGTHWISE, GRID_CROSSWISE), jnp.float32) ** levels(arg_keys[3], (LAMINA_TOTAL, GRID_LENGTHWISE, GRID_CROSSWISE), ((0, 16), (1, 32)), -0.2, 0.2)), 0.02, 0.2)
    wetted_flags = plant((jax.random.randint(arg_keys[4], (LAMINA_TOTAL, GRID_LENGTHWISE, GRID_CROSSWISE), 0, 4) < 3).astype(jnp.int32), jax.random.fold_in(arg_keys[4], 1), 0, 1)
    injection_flags = plant((jax.random.randint(arg_keys[5], (LAMINA_TOTAL, GRID_LENGTHWISE, GRID_CROSSWISE), 0, 32) < 1).astype(jnp.int32), jax.random.fold_in(arg_keys[5], 1), 0, 1)
    outlet_flags = plant((jax.random.randint(arg_keys[6], (LAMINA_TOTAL, GRID_LENGTHWISE, GRID_CROSSWISE), 0, 32) < 1).astype(jnp.int32), jax.random.fold_in(arg_keys[6], 1), 0, 1)
    return dict(scaled_warmth=scaled_warmth, crosslink_fraction=crosslink_fraction, fluid_stress=fluid_stress, preform_porosity_coefficient=preform_porosity_coefficient, wetted_flags=wetted_flags, injection_flags=injection_flags, outlet_flags=outlet_flags)


fluidity_barrier = 4.0
fluidity_gelation_coefficient = 2.0
arrhenius_prefactor = 0.2
arrhenius_barrier = 8.0
released_enthalpy = 0.3
diffusion_coefficient = 0.1
clock_step_size = 0.5
epsilon = 1e-06

def interior(array):
    return array[1:-1, 1:-1, 1:-1]

def nearby_sites(array):
    return [array[2:, 1:-1, 1:-1], array[:-2, 1:-1, 1:-1], array[1:-1, 2:, 1:-1], array[1:-1, :-2, 1:-1], array[1:-1, 1:-1, 2:], array[1:-1, 1:-1, :-2]]

def face_mobility(mobility_pad):
    centre = interior(mobility_pad)
    result = []
    for beside in nearby_sites(mobility_pad):
        denom = centre + beside
        result.append(2.0 * centre * beside / jnp.where(denom > 0, denom, 1.0))
    return result

def jacobi_sweep(pressure_pad, boundary_sides, dry_site, fixed_value):
    beside = nearby_sites(pressure_pad)
    weighted = boundary_sides[0] * beside[0]
    diagonal_sum = boundary_sides[0]
    for iteration_counter in range(1, 6):
        weighted = weighted + boundary_sides[iteration_counter] * beside[iteration_counter]
        diagonal_sum = diagonal_sum + boundary_sides[iteration_counter]
    return jnp.where(dry_site > 0, weighted / jnp.where(dry_site > 0, diagonal_sum, 1.0), fixed_value)

def donor_advection(fluid_stress, scaled_warmth, crosslink_fraction, boundary_sides, nearby_stress, nearby_warmth, nearby_crosslink, wetted_status, nearby_wetted, dry_site):
    weighted = boundary_sides[0] * nearby_stress[0]
    diagonal_sum = boundary_sides[0]
    for iteration_counter in range(1, 6):
        weighted = weighted + boundary_sides[iteration_counter] * nearby_stress[iteration_counter]
        diagonal_sum = diagonal_sum + boundary_sides[iteration_counter]
    darcy_imbalance = dry_site * (weighted - diagonal_sum * fluid_stress)
    donor_warmth_advance = jnp.zeros_like(scaled_warmth)
    donor_crosslink_advance = jnp.zeros_like(scaled_warmth)
    diffusive_stream = jnp.zeros_like(scaled_warmth)
    for iteration_counter in range(6):
        inward_stream = jnp.maximum(boundary_sides[iteration_counter] * (nearby_stress[iteration_counter] - fluid_stress), 0.0) * nearby_wetted[iteration_counter]
        donor_warmth_advance = donor_warmth_advance + inward_stream * (nearby_warmth[iteration_counter] - scaled_warmth)
        donor_crosslink_advance = donor_crosslink_advance + inward_stream * (nearby_crosslink[iteration_counter] - crosslink_fraction)
        diffusive_stream = diffusive_stream + nearby_wetted[iteration_counter] * (nearby_warmth[iteration_counter] - scaled_warmth)
    crosslink_speed = arrhenius_prefactor * jnp.exp(arrhenius_barrier * (1.0 - 1.0 / scaled_warmth)) * (1.0 - crosslink_fraction)
    advanced_warmth = scaled_warmth + wetted_status * clock_step_size * (donor_warmth_advance + diffusion_coefficient * diffusive_stream + released_enthalpy * crosslink_speed)
    advanced_crosslink = crosslink_fraction + wetted_status * clock_step_size * (donor_crosslink_advance + crosslink_speed)
    return (darcy_imbalance, advanced_warmth, advanced_crosslink)

def reference(scaled_warmth, crosslink_fraction, fluid_stress, preform_porosity_coefficient, wetted_flags, injection_flags, outlet_flags):
    wetted_status = wetted_flags.astype(jnp.float32)
    inlet_cell = injection_flags.astype(jnp.float32)
    dry_site = wetted_status * (1.0 - inlet_cell) * (1.0 - outlet_flags.astype(jnp.float32))
    nearby_wetted = nearby_sites(jnp.pad(wetted_status, 1))
    gathered_magnitudes = []
    for repeat in range(STEPS):
        fluid_conductance = preform_porosity_coefficient * jnp.exp(-(fluidity_barrier * (1.0 / scaled_warmth - 1.0) + fluidity_gelation_coefficient * crosslink_fraction))
        boundary_sides = face_mobility(jnp.pad(fluid_conductance, 1))
        for sweep_index in range(SWEEPS):
            fluid_stress = jacobi_sweep(jnp.pad(fluid_stress, 1), boundary_sides, dry_site, inlet_cell)
        darcy_imbalance, scaled_warmth, crosslink_fraction = donor_advection(fluid_stress, scaled_warmth, crosslink_fraction, boundary_sides, nearby_sites(jnp.pad(fluid_stress, 1)), nearby_sites(jnp.pad(scaled_warmth, 1)), nearby_sites(jnp.pad(crosslink_fraction, 1)), wetted_status, nearby_wetted, dry_site)
        gathered_magnitudes.append(jnp.sqrt(jnp.sum(darcy_imbalance * darcy_imbalance) / darcy_imbalance.size + epsilon))
    return (scaled_warmth, crosslink_fraction, fluid_stress, jnp.stack(gathered_magnitudes))
```

```python
import jax
import jax.numpy as jnp
from jax import lax
from jax.sharding import PartitionSpec as P


STEPS = 2
SWEEPS = 4


fluidity_barrier = 4.0
fluidity_gelation_coefficient = 2.0
arrhenius_prefactor = 0.2
arrhenius_barrier = 8.0
released_enthalpy = 0.3
diffusion_coefficient = 0.1
clock_step_size = 0.5
epsilon = 1e-06


def swap_pairs(count, parity):
    pairs = []
    for i in range(parity, count - 1, 2):
        pairs += [(i, i + 1), (i + 1, i)]
    return pairs


def trade_faces(array):
    ply_even = lax.axis_index("ply") % 2 == 0
    tile_even = lax.axis_index("tile") % 2 == 0
    first_ply, last_ply = array[:, :1], array[:, -1:]
    first_row, last_row = array[:, :, :1], array[:, :, -1:]
    sends = lax.optimization_barrier(
        (
            jnp.where(ply_even, first_ply, last_ply),
            jnp.where(ply_even, last_ply, first_ply),
            jnp.where(tile_even, first_row, last_row),
            jnp.where(tile_even, last_row, first_row),
        )
    )
    nply, ntile = lax.axis_size("ply"), lax.axis_size("tile")
    ply_odd = lax.ppermute(sends[0], "ply", swap_pairs(nply, 1))
    ply_pair = lax.ppermute(sends[1], "ply", swap_pairs(nply, 0))
    tile_odd = lax.ppermute(sends[2], "tile", swap_pairs(ntile, 1))
    tile_pair = lax.ppermute(sends[3], "tile", swap_pairs(ntile, 0))
    return (
        jnp.where(ply_even, ply_pair, ply_odd),
        jnp.where(ply_even, ply_odd, ply_pair),
        jnp.where(tile_even, tile_pair, tile_odd),
        jnp.where(tile_even, tile_odd, tile_pair),
    )


def nearby_sites(array, faces):
    edge = jnp.zeros_like(array[:, :, :1])
    return [
        jnp.concatenate([array[1:], faces[0]], axis=0),
        jnp.concatenate([faces[1], array[:-1]], axis=0),
        jnp.concatenate([array[:, 1:], faces[2]], axis=1),
        jnp.concatenate([faces[3], array[:, :-1]], axis=1),
        jnp.concatenate([array[:, :, 1:], edge], axis=2),
        jnp.concatenate([edge, array[:, :, :-1]], axis=2),
    ]


def face_mobility(centre, nearby):
    result = []
    for beside in nearby:
        denom = centre + beside
        result.append(2.0 * centre * beside / jnp.where(denom > 0, denom, 1.0))
    return result


def jacobi_sweep(beside, boundary_sides, dry_site, fixed_value):
    weighted = boundary_sides[0] * beside[0]
    diagonal_sum = boundary_sides[0]
    for iteration_counter in range(1, 6):
        weighted = weighted + boundary_sides[iteration_counter] * beside[iteration_counter]
        diagonal_sum = diagonal_sum + boundary_sides[iteration_counter]
    return jnp.where(
        dry_site > 0, weighted / jnp.where(dry_site > 0, diagonal_sum, 1.0), fixed_value
    )


def donor_advection(
    fluid_stress,
    scaled_warmth,
    crosslink_fraction,
    boundary_sides,
    nearby_stress,
    nearby_warmth,
    nearby_crosslink,
    wetted_status,
    nearby_wetted,
    dry_site,
):
    weighted = boundary_sides[0] * nearby_stress[0]
    diagonal_sum = boundary_sides[0]
    for iteration_counter in range(1, 6):
        weighted = weighted + boundary_sides[iteration_counter] * nearby_stress[iteration_counter]
        diagonal_sum = diagonal_sum + boundary_sides[iteration_counter]
    darcy_imbalance = dry_site * (weighted - diagonal_sum * fluid_stress)
    donor_warmth_advance = jnp.zeros_like(scaled_warmth)
    donor_crosslink_advance = jnp.zeros_like(scaled_warmth)
    diffusive_stream = jnp.zeros_like(scaled_warmth)
    for iteration_counter in range(6):
        inward_stream = (
            jnp.maximum(
                boundary_sides[iteration_counter]
                * (nearby_stress[iteration_counter] - fluid_stress),
                0.0,
            )
            * nearby_wetted[iteration_counter]
        )
        donor_warmth_advance = donor_warmth_advance + inward_stream * (
            nearby_warmth[iteration_counter] - scaled_warmth
        )
        donor_crosslink_advance = donor_crosslink_advance + inward_stream * (
            nearby_crosslink[iteration_counter] - crosslink_fraction
        )
        diffusive_stream = diffusive_stream + nearby_wetted[iteration_counter] * (
            nearby_warmth[iteration_counter] - scaled_warmth
        )
    crosslink_speed = (
        arrhenius_prefactor
        * jnp.exp(arrhenius_barrier * (1.0 - 1.0 / scaled_warmth))
        * (1.0 - crosslink_fraction)
    )
    advanced_warmth = scaled_warmth + wetted_status * clock_step_size * (
        donor_warmth_advance
        + diffusion_coefficient * diffusive_stream
        + released_enthalpy * crosslink_speed
    )
    advanced_crosslink = crosslink_fraction + wetted_status * clock_step_size * (
        donor_crosslink_advance + crosslink_speed
    )
    return (darcy_imbalance, advanced_warmth, advanced_crosslink)


def per_device(
    scaled_warmth,
    crosslink_fraction,
    fluid_stress,
    preform_porosity_coefficient,
    wetted_flags,
    injection_flags,
    outlet_flags,
):
    wetted_status = wetted_flags.astype(jnp.float32)
    inlet_cell = injection_flags.astype(jnp.float32)
    dry_site = wetted_status * (1.0 - inlet_cell) * (1.0 - outlet_flags.astype(jnp.float32))
    devices = lax.axis_size("ply") * lax.axis_size("tile")
    site_total = scaled_warmth.size * devices
    nearby_wetted = None
    local_sums = []
    for _ in range(STEPS):
        fluid_conductance = preform_porosity_coefficient * jnp.exp(
            -(
                fluidity_barrier * (1.0 / scaled_warmth - 1.0)
                + fluidity_gelation_coefficient * crosslink_fraction
            )
        )
        fields = [fluid_stress, fluid_conductance, scaled_warmth, crosslink_fraction]
        if nearby_wetted is None:
            fields.append(wetted_status)
        faces = trade_faces(jnp.stack(fields))
        nearby = [
            nearby_sites(field, [face[k] for face in faces]) for k, field in enumerate(fields)
        ]
        nearby_stress, nearby_mobility, nearby_warmth, nearby_crosslink = nearby[:4]
        if nearby_wetted is None:
            nearby_wetted = nearby[4]
        boundary_sides = face_mobility(fluid_conductance, nearby_mobility)
        for _ in range(SWEEPS):
            fluid_stress = jacobi_sweep(nearby_stress, boundary_sides, dry_site, inlet_cell)
            faces = trade_faces(fluid_stress[None])
            nearby_stress = nearby_sites(fluid_stress, [face[0] for face in faces])
        darcy_imbalance, scaled_warmth, crosslink_fraction = donor_advection(
            fluid_stress,
            scaled_warmth,
            crosslink_fraction,
            boundary_sides,
            nearby_stress,
            nearby_warmth,
            nearby_crosslink,
            wetted_status,
            nearby_wetted,
            dry_site,
        )
        local_sums.append(jnp.sum(darcy_imbalance * darcy_imbalance))
    lane = lax.broadcasted_iota(jnp.int32, (devices, 1, 128), 2)
    message = jnp.where(lane == 0, local_sums[0], jnp.where(lane == 1, local_sums[1], 0.0))
    parts = lax.all_to_all(message, ("ply", "tile"), 0, 0)
    totals = jnp.sum(parts, axis=(0, 1))[:STEPS]
    imbalance_record = jnp.sqrt(totals / site_total + epsilon)
    return (scaled_warmth, crosslink_fraction, fluid_stress, imbalance_record)


def solution(mesh):
    return jax.shard_map(
        per_device,
        mesh=mesh,
        in_specs=(
            P("ply", "tile", None),
            P("ply", "tile", None),
            P("ply", "tile", None),
            P("ply", "tile", None),
            P("ply", "tile", None),
            P("ply", "tile", None),
            P("ply", "tile", None),
        ),
        out_specs=(P("ply", "tile", None), P("ply", "tile", None), P("ply", "tile", None), P()),
        check_vma=False,
    )
```

```python
import jax
import jax.numpy as jnp
from jax import lax
from jax.sharding import PartitionSpec as P


STEPS = 2
SWEEPS = 4


fluidity_barrier = 4.0
fluidity_gelation_coefficient = 2.0
arrhenius_prefactor = 0.2
arrhenius_barrier = 8.0
released_enthalpy = 0.3
diffusion_coefficient = 0.1
clock_step_size = 0.5
epsilon = 1e-06


def swap_pairs(count, parity):
    pairs = []
    for i in range(parity, count - 1, 2):
        pairs += [(i, i + 1), (i + 1, i)]
    return pairs


def trade_faces(array):
    ply_even = lax.axis_index("ply") % 2 == 0
    tile_even = lax.axis_index("tile") % 2 == 0
    first_ply, last_ply = array[:, :1], array[:, -1:]
    first_row, last_row = array[:, :, :1], array[:, :, -1:]
    sends = lax.optimization_barrier(
        (
            jnp.where(ply_even, first_ply, last_ply),
            jnp.where(ply_even, last_ply, first_ply),
            jnp.where(tile_even, first_row, last_row),
            jnp.where(tile_even, last_row, first_row),
        )
    )
    nply, ntile = lax.axis_size("ply"), lax.axis_size("tile")
    ply_odd = lax.ppermute(sends[0], "ply", swap_pairs(nply, 1))
    ply_pair = lax.ppermute(sends[1], "ply", swap_pairs(nply, 0))
    tile_odd = lax.ppermute(sends[2], "tile", swap_pairs(ntile, 1))
    tile_pair = lax.ppermute(sends[3], "tile", swap_pairs(ntile, 0))
    return (
        jnp.where(ply_even, ply_pair, ply_odd),
        jnp.where(ply_even, ply_odd, ply_pair),
        jnp.where(tile_even, tile_pair, tile_odd),
        jnp.where(tile_even, tile_odd, tile_pair),
    )


def nearby_sites(array, faces):
    edge = jnp.zeros_like(array[:, :, :1])
    return [
        jnp.concatenate([array[1:], faces[0]], axis=0),
        jnp.concatenate([faces[1], array[:-1]], axis=0),
        jnp.concatenate([array[:, 1:], faces[2]], axis=1),
        jnp.concatenate([faces[3], array[:, :-1]], axis=1),
        jnp.concatenate([array[:, :, 1:], edge], axis=2),
        jnp.concatenate([edge, array[:, :, :-1]], axis=2),
    ]


def trade(*fields):
    faces = trade_faces(jnp.stack(fields))
    return [nearby_sites(field, [face[k] for face in faces]) for k, field in enumerate(fields)]


def face_mobility(centre, nearby):
    result = []
    for beside in nearby:
        denom = centre + beside
        result.append(2.0 * centre * beside / jnp.where(denom > 0, denom, 1.0))
    return result


def jacobi_sweep(beside, boundary_sides, dry_site, fixed_value):
    weighted = boundary_sides[0] * beside[0]
    diagonal_sum = boundary_sides[0]
    for iteration_counter in range(1, 6):
        weighted = weighted + boundary_sides[iteration_counter] * beside[iteration_counter]
        diagonal_sum = diagonal_sum + boundary_sides[iteration_counter]
    return jnp.where(
        dry_site > 0, weighted / jnp.where(dry_site > 0, diagonal_sum, 1.0), fixed_value
    )


def donor_advection(
    fluid_stress,
    scaled_warmth,
    crosslink_fraction,
    boundary_sides,
    nearby_stress,
    nearby_warmth,
    nearby_crosslink,
    wetted_status,
    nearby_wetted,
    dry_site,
):
    weighted = boundary_sides[0] * nearby_stress[0]
    diagonal_sum = boundary_sides[0]
    for iteration_counter in range(1, 6):
        weighted = weighted + boundary_sides[iteration_counter] * nearby_stress[iteration_counter]
        diagonal_sum = diagonal_sum + boundary_sides[iteration_counter]
    darcy_imbalance = dry_site * (weighted - diagonal_sum * fluid_stress)
    donor_warmth_advance = jnp.zeros_like(scaled_warmth)
    donor_crosslink_advance = jnp.zeros_like(scaled_warmth)
    diffusive_stream = jnp.zeros_like(scaled_warmth)
    for iteration_counter in range(6):
        inward_stream = (
            jnp.maximum(
                boundary_sides[iteration_counter]
                * (nearby_stress[iteration_counter] - fluid_stress),
                0.0,
            )
            * nearby_wetted[iteration_counter]
        )
        donor_warmth_advance = donor_warmth_advance + inward_stream * (
            nearby_warmth[iteration_counter] - scaled_warmth
        )
        donor_crosslink_advance = donor_crosslink_advance + inward_stream * (
            nearby_crosslink[iteration_counter] - crosslink_fraction
        )
        diffusive_stream = diffusive_stream + nearby_wetted[iteration_counter] * (
            nearby_warmth[iteration_counter] - scaled_warmth
        )
    crosslink_speed = (
        arrhenius_prefactor
        * jnp.exp(arrhenius_barrier * (1.0 - 1.0 / scaled_warmth))
        * (1.0 - crosslink_fraction)
    )
    advanced_warmth = scaled_warmth + wetted_status * clock_step_size * (
        donor_warmth_advance
        + diffusion_coefficient * diffusive_stream
        + released_enthalpy * crosslink_speed
    )
    advanced_crosslink = crosslink_fraction + wetted_status * clock_step_size * (
        donor_crosslink_advance + crosslink_speed
    )
    return (darcy_imbalance, advanced_warmth, advanced_crosslink)


def per_device(
    scaled_warmth,
    crosslink_fraction,
    fluid_stress,
    preform_porosity_coefficient,
    wetted_flags,
    injection_flags,
    outlet_flags,
):
    wetted_status = wetted_flags.astype(jnp.float32)
    inlet_cell = injection_flags.astype(jnp.float32)
    dry_site = wetted_status * (1.0 - inlet_cell) * (1.0 - outlet_flags.astype(jnp.float32))
    devices = lax.axis_size("ply") * lax.axis_size("tile")
    site_total = scaled_warmth.size * devices
    nearby_wetted = nearby_stress = None
    local_sums = []
    for _ in range(STEPS):
        fluid_conductance = preform_porosity_coefficient * jnp.exp(
            -(
                fluidity_barrier * (1.0 / scaled_warmth - 1.0)
                + fluidity_gelation_coefficient * crosslink_fraction
            )
        )
        if nearby_stress is None:
            nearby_mobility, nearby_stress = trade(fluid_conductance, fluid_stress)
            riders = [scaled_warmth, crosslink_fraction, wetted_status]
            arrived = []
        else:
            nearby_mobility, nearby_warmth = trade(fluid_conductance, scaled_warmth)
            riders = [crosslink_fraction]
            arrived = [nearby_warmth]
        boundary_sides = face_mobility(fluid_conductance, nearby_mobility)
        for sweep_index in range(SWEEPS):
            fluid_stress = jacobi_sweep(nearby_stress, boundary_sides, dry_site, inlet_cell)
            rider = riders[sweep_index : sweep_index + 1]
            nearby_stress, *rest = trade(fluid_stress, *rider)
            arrived += rest
        nearby_warmth, nearby_crosslink = arrived[:2]
        if nearby_wetted is None:
            nearby_wetted = arrived[2]
        darcy_imbalance, scaled_warmth, crosslink_fraction = donor_advection(
            fluid_stress,
            scaled_warmth,
            crosslink_fraction,
            boundary_sides,
            nearby_stress,
            nearby_warmth,
            nearby_crosslink,
            wetted_status,
            nearby_wetted,
            dry_site,
        )
        local_sums.append(jnp.sum(darcy_imbalance * darcy_imbalance))
    lane = lax.broadcasted_iota(jnp.int32, (devices, 1, 128), 2)
    message = jnp.where(lane == 0, local_sums[0], jnp.where(lane == 1, local_sums[1], 0.0))
    parts = lax.all_to_all(message, ("ply", "tile"), 0, 0)
    totals = jnp.sum(parts, axis=(0, 1))[:STEPS]
    imbalance_record = jnp.sqrt(totals / site_total + epsilon)
    return (scaled_warmth, crosslink_fraction, fluid_stress, imbalance_record)


def solution(mesh):
    return jax.shard_map(
        per_device,
        mesh=mesh,
        in_specs=(
            P("ply", "tile", None),
            P("ply", "tile", None),
            P("ply", "tile", None),
            P("ply", "tile", None),
            P("ply", "tile", None),
            P("ply", "tile", None),
            P("ply", "tile", None),
        ),
        out_specs=(P("ply", "tile", None), P("ply", "tile", None), P("ply", "tile", None), P()),
        check_vma=False,
    )
```

```python
import functools

import jax
import jax.numpy as jnp
from jax import lax
from jax.experimental import pallas as pl
from jax.experimental.pallas import tpu as pltpu
from jax.sharding import PartitionSpec as P


STEPS = 2


fluidity_barrier = 4.0
fluidity_gelation_coefficient = 2.0
arrhenius_prefactor = 0.2
arrhenius_barrier = 8.0
released_enthalpy = 0.3
diffusion_coefficient = 0.1
clock_step_size = 0.5
epsilon = 1e-06

PLIES, ROWS, SUB, LANE = 4, 8, 8, 128
OFF = 3
DEEP = (PLIES + 2 * OFF, ROWS + 2 * OFF, SUB, LANE)
RIM = (PLIES + 2, ROWS + 2, SUB, LANE)
BLOCK = (PLIES, ROWS, SUB, LANE)


def swap_pairs(count, parity):
    pairs = []
    for i in range(parity, count - 1, 2):
        pairs += [(i, i + 1), (i + 1, i)]
    return pairs


def swap(axis, odd_send, even_send):
    count = lax.axis_size(axis)
    odd = lax.ppermute(odd_send, axis, swap_pairs(count, 1))
    even = lax.ppermute(even_send, axis, swap_pairs(count, 0))
    return odd, even


def cell_index(shape):
    return LANE * lax.broadcasted_iota(jnp.int32, shape, 1) + lax.broadcasted_iota(
        jnp.int32, shape, 2
    )


def next_cell(x):
    moved = pltpu.roll(x, LANE - 1, 2)
    lane = lax.broadcasted_iota(jnp.int32, x.shape, 2)
    return jnp.where(lane == LANE - 1, pltpu.roll(moved, SUB - 1, 1), moved)


def previous_cell(x):
    moved = pltpu.roll(x, 1, 2)
    lane = lax.broadcasted_iota(jnp.int32, x.shape, 2)
    return jnp.where(lane == 0, pltpu.roll(moved, 1, 1), moved)


def beside(ref, i, top, end, walled=False):
    centre = ref[i, top:end]
    after, before = next_cell(centre), previous_cell(centre)
    if walled:
        cell = cell_index(centre.shape)
        after = jnp.where(cell == SUB * LANE - 1, 0.0, after)
        before = jnp.where(cell == 0, 0.0, before)
    return centre, [
        ref[i + 1, top:end],
        ref[i - 1, top:end],
        ref[i, top + 1 : end + 1],
        ref[i, top - 1 : end - 1],
        after,
        before,
    ]


def face_list(mobility, i, top, end):
    centre, around = beside(mobility, i, top, end, walled=True)
    result = []
    for other in around:
        denom = centre + other
        result.append(2.0 * centre * other / jnp.where(denom > 0, denom, 1.0))
    return result


def mobility_of(preform, warmth, crosslink):
    return preform * jnp.exp(
        -(
            fluidity_barrier * (1.0 / warmth - 1.0)
            + fluidity_gelation_coefficient * crosslink
        )
    )


def loop(count, body):
    def step(i, carry):
        body(i)
        return carry

    lax.fori_loop(0, count, step, 0)


def pack_plies(par, local, depth, odd_out, even_out, unit):
    last = PLIES - depth
    odd_out[unit : unit + depth] = local[pl.ds(par[0] * last, depth)]
    even_out[unit : unit + depth] = local[pl.ds((1 - par[0]) * last, depth)]


def pack_rows(par, local, odd_in, even_in, unit, depth, odd_out, even_out, base, corners=True):
    last = ROWS - depth
    for out, start in ((odd_out, par[1] * last), (even_out, (1 - par[1]) * last)):
        skip = depth if corners else 0
        for i in range(PLIES):
            at = base + (skip + i) * depth
            out[at : at + depth] = local[i, pl.ds(start, depth)]
        if corners:
            for came, first in (
                (odd_in, par[0] * (PLIES + depth)),
                (even_in, (1 - par[0]) * (PLIES + depth)),
            ):
                for i in range(depth):
                    out[pl.ds(base + (first + i) * depth, depth)] = came[
                        unit + i, pl.ds(start, depth)
                    ]


def assemble(par, dst, off, local, ply_in, unit, row_in, base, depth, corners=True):
    for i in range(PLIES):
        dst[off + i, off : off + ROWS] = local[i]
    for came, side in zip(ply_in, (par[0], 1 - par[0]), strict=True):
        first = off - depth + side * (PLIES + depth)
        for i in range(depth):
            dst[first + i, off : off + ROWS] = came[unit + i]
    skip = 0 if corners else depth
    for came, side in zip(row_in, (par[1], 1 - par[1]), strict=True):
        first = off - depth + side * (ROWS + depth)
        for i in range(PLIES + 2 * (depth - skip)):
            at = base + i * depth
            dst[off - depth + skip + i, pl.ds(first, depth)] = came[at : at + depth]


def to_lines(flat, lines, i):
    for j in range(SUB):
        part = flat[i, :, j * LANE : (j + 1) * LANE].astype(jnp.float32)
        lines[pl.ds(j, ROWS, stride=SUB), :] = part
    return lines[...].reshape(ROWS, SUB, LANE)


def from_lines(value, lines, flat, i):
    lines[...] = value.reshape(ROWS * SUB, LANE)
    for j in range(SUB):
        flat[i, :, j * LANE : (j + 1) * LANE] = lines[pl.ds(j, ROWS, stride=SUB), :]


def prepare_kernel(
    par, warmth, crosslink, stress, preform, wetted, inlet, outlet,
    warmth_out, crosslink_out, stress_out, preform_out, mobility, free, fixed, fill,
    odd_out, even_out, *lines,
):
    for i in range(PLIES):
        t = to_lines(warmth, lines[0], i)
        c = to_lines(crosslink, lines[1], i)
        k = to_lines(preform, lines[2], i)
        warmth_out[i] = t
        crosslink_out[i] = c
        preform_out[i] = k
        mobility[i] = mobility_of(k, t, c)
        stress_out[i] = to_lines(stress, lines[3], i)
        w = to_lines(wetted, lines[4], i)
        n = to_lines(inlet, lines[5], i)
        o = to_lines(outlet, lines[6], i)
        fill[i] = w
        fixed[i] = n
        free[i] = w * (1.0 - n) * (1.0 - o)
    pack_plies(par, stress_out, 3, odd_out, even_out, 0)
    pack_plies(par, mobility, 3, odd_out, even_out, 3)
    pack_plies(par, free, 2, odd_out, even_out, 6)
    pack_plies(par, fixed, 2, odd_out, even_out, 8)


FIRST = ((0, 0, 3), (3, 30, 3), (6, 60, 2), (8, 76, 2))


def rows_kernel(layout, corners, par, *refs):
    n = len(layout)
    odd_in, even_in, odd_out, even_out = refs[n:]
    for local, (unit, base, depth), corner in zip(refs[:n], layout, corners, strict=True):
        pack_rows(par, local, odd_in, even_in, unit, depth, odd_out, even_out, base, corner)


def sweep(source, target, weights, shift, depth):
    top, end = OFF - depth, OFF + ROWS + depth

    def ply(k):
        i = OFF - depth + k
        _, around = beside(source, i, top, end)
        rows = slice(top - shift, end - shift)
        total = weights[6, i - shift, rows]
        for f in range(6):
            total = total + weights[f, i - shift, rows] * around[f]
        target[i, top:end] = total

    loop(PLIES + 2 * depth, ply)


def sweeps_kernel(first, par, *refs):
    if first:
        (stress, mobility, free, fixed, warmth, crosslink, fill,
         odd_in, even_in, odd_rows, even_rows,
         stress_out, weights_out, mobility_out, free_deep, fixed_deep, odd_out, even_out,
         p0, p1, m, weights) = refs
    else:
        (stress, mobility, free_deep, fixed_deep, warmth, crosslink,
         odd_in, even_in, odd_rows, even_rows,
         stress_out, weights_out, mobility_out, odd_out, even_out,
         p0, p1, m, weights) = refs
    fields = [(p0, stress), (m, mobility)]
    if first:
        fields += [(free_deep, free), (fixed_deep, fixed)]
    for (dst, local), (unit, base, depth) in zip(fields, FIRST, strict=False):
        assemble(par, dst, OFF, local, (odd_in, even_in), unit, (odd_rows, even_rows), base, depth)
    top, end = 1, OFF + ROWS + 2

    def weigh(k):
        i = 1 + k
        faces = face_list(m, i, top, end)
        is_free = free_deep[i, top:end] > 0
        total = faces[0]
        for f in range(1, 6):
            total = total + faces[f]
        scale = jnp.where(is_free, 1.0 / jnp.where(is_free, total, 1.0), 0.0)
        for f in range(6):
            weights[f, k] = faces[f] * scale
        weights[6, k] = jnp.where(is_free, 0.0, fixed_deep[i, top:end])

    loop(PLIES + 4, weigh)
    sweep(p0, p1, weights, 1, 2)
    sweep(p1, p0, weights, 1, 1)
    sweep(p0, p1, weights, 1, 0)
    for i in range(PLIES):
        stress_out[i] = p1[OFF + i, OFF : OFF + ROWS]

    def keep(k):
        mobility_out[k] = m[k + OFF - 1, OFF - 1 : OFF + ROWS + 1]
        for f in range(7):
            weights_out[f, k] = weights[f, k + 1, 1 : 1 + ROWS + 2]

    loop(PLIES + 2, keep)
    pack_plies(par, stress_out, 2, odd_out, even_out, 0)
    pack_plies(par, warmth, 1, odd_out, even_out, 2)
    pack_plies(par, crosslink, 1, odd_out, even_out, 3)
    if first:
        pack_plies(par, fill, 1, odd_out, even_out, 4)


SECOND = ((0, 0, 2), (2, 16, 1), (3, 20, 1), (4, 24, 1))


def residual_kernel(
    par, stress, weights, mobility, free, odd_in, even_in, odd_rows, even_rows,
    stress_rim, squares, p0, p1,
):
    assemble(par, p0, OFF, stress, (odd_in, even_in), 0, (odd_rows, even_rows), 0, 2)
    sweep(p0, p1, weights, OFF - 1, 1)
    squares[...] = jnp.zeros((SUB, LANE), jnp.float32)

    def ply(k):
        centre, around = beside(p1, OFF + k, OFF, OFF + ROWS)
        faces = face_list(mobility, 1 + k, 1, 1 + ROWS)
        weighted = faces[0] * around[0]
        total = faces[0]
        for f in range(1, 6):
            weighted = weighted + faces[f] * around[f]
            total = total + faces[f]
        imbalance = free[k] * (weighted - total * centre)
        squares[...] += jnp.sum(imbalance * imbalance, axis=0)

    loop(PLIES, ply)

    def keep(k):
        stress_rim[k] = p1[k + OFF - 1, OFF - 1 : OFF + ROWS + 1]

    loop(PLIES + 2, keep)


def transport_kernel(first, last, par, *refs):
    stress_rim, mobility, warmth, crosslink, preform = refs[:5]
    if first:
        fill, refs = refs[5], refs[6:]
    else:
        fill_rim, refs = refs[5], refs[6:]
    odd_in, even_in, odd_rows, even_rows = refs[:4]
    refs = refs[4:]
    if last:
        warmth_out, crosslink_out, stress_out = refs[:3]
        refs = refs[3:]
    else:
        warmth_out, crosslink_out, stress_out, mobility_out, odd_out, even_out = refs[:6]
        refs = refs[6:]
    if first:
        fill_rim, refs = refs[0], refs[1:]
    t_rim, c_rim = refs[:2]
    lines = refs[2:]
    fields = [(t_rim, warmth), (c_rim, crosslink)]
    if first:
        fields.append((fill_rim, fill))
    for (dst, local), (unit, base, depth) in zip(fields, SECOND[1:], strict=False):
        assemble(
            par, dst, 1, local, (odd_in, even_in), unit, (odd_rows, even_rows), base, depth, False
        )

    def ply(k):
        i, top, end = 1 + k, 1, 1 + ROWS
        stress, near_stress = beside(stress_rim, i, top, end)
        t, near_t = beside(t_rim, i, top, end)
        c, near_c = beside(c_rim, i, top, end)
        full, near_full = beside(fill_rim, i, top, end, walled=True)
        faces = face_list(mobility, i, top, end)
        t_gain = jnp.zeros_like(t)
        c_gain = jnp.zeros_like(t)
        spread = jnp.zeros_like(t)
        for f in range(6):
            inward = jnp.maximum(faces[f] * (near_stress[f] - stress), 0.0) * near_full[f]
            t_step = near_t[f] - t
            t_gain = t_gain + inward * t_step
            c_gain = c_gain + inward * (near_c[f] - c)
            spread = spread + near_full[f] * t_step
        speed = (
            arrhenius_prefactor * jnp.exp(arrhenius_barrier * (1.0 - 1.0 / t)) * (1.0 - c)
        )
        t_new = t + full * clock_step_size * (
            t_gain + diffusion_coefficient * spread + released_enthalpy * speed
        )
        c_new = c + full * clock_step_size * (c_gain + speed)
        if last:
            from_lines(t_new, lines[0], warmth_out, k)
            from_lines(c_new, lines[1], crosslink_out, k)
            from_lines(stress, lines[2], stress_out, k)
        else:
            warmth_out[k] = t_new
            crosslink_out[k] = c_new
            stress_out[k] = stress
            mobility_out[k] = mobility_of(preform[k], t_new, c_new)

    if last:
        for k in range(PLIES):
            ply(k)
    else:
        loop(PLIES, ply)
        pack_plies(par, stress_out, 3, odd_out, even_out, 0)
        pack_plies(par, mobility_out, 3, odd_out, even_out, 3)


def call(kernel, args, outs, scratch=()):
    vmem = pl.BlockSpec(memory_space=pltpu.VMEM)
    return pl.pallas_call(
        kernel,
        out_shape=[jax.ShapeDtypeStruct(shape, jnp.float32) for shape in outs],
        in_specs=[pl.BlockSpec(memory_space=pltpu.SMEM)] + [vmem] * (len(args) - 1),
        out_specs=[vmem] * len(outs),
        scratch_shapes=[pltpu.VMEM(shape, jnp.float32) for shape in scratch],
    )(*args)


def exchange(par, fields, layout, corners, sends):
    came = swap("ply", *sends)
    lines = sum(
        (PLIES + (2 * depth if corner else 0)) * depth
        for (_, _, depth), corner in zip(layout, corners, strict=True)
    )
    rows = call(
        functools.partial(rows_kernel, layout, corners),
        [par, *fields, *came],
        [(lines, SUB, LANE)] * 2,
    )
    return (*came, *swap("tile", *rows))


def per_device(
    scaled_warmth,
    crosslink_fraction,
    fluid_stress,
    preform_porosity_coefficient,
    wetted_flags,
    injection_flags,
    outlet_flags,
):
    devices = lax.axis_size("ply") * lax.axis_size("tile")
    site_total = scaled_warmth.size * devices
    shape = scaled_warmth.shape
    assert shape == (PLIES, ROWS, SUB * LANE)
    pair = lax.broadcasted_iota(jnp.int32, (2,), 0)
    par = jnp.where(pair == 0, lax.axis_index("ply") % 2, lax.axis_index("tile") % 2)
    line = (ROWS * SUB, LANE)
    (warmth, crosslink, stress, preform, mobility, free, fixed, fill, *sends) = call(
        prepare_kernel,
        [
            par,
            scaled_warmth,
            crosslink_fraction,
            fluid_stress,
            preform_porosity_coefficient,
            wetted_flags,
            injection_flags,
            outlet_flags,
        ],
        [BLOCK] * 8 + [(10, ROWS, SUB, LANE)] * 2,
        [line] * 7,
    )
    local_sums = []
    for repeat in range(STEPS):
        first, last = repeat == 0, repeat == STEPS - 1
        fields = [stress, mobility] + ([free, fixed] if first else [])
        count = len(fields)
        came = exchange(par, fields, FIRST[:count], (True,) * count, sends)
        units = 5 if first else 4
        args = fields if first else fields + [free_deep, fixed_deep]
        result = call(
            functools.partial(sweeps_kernel, first),
            [par, *args, warmth, crosslink, *([fill] if first else []), *came],
            [BLOCK, (7, *RIM), RIM]
            + ([DEEP] * 2 if first else [])
            + [(units, ROWS, SUB, LANE)] * 2,
            [DEEP, DEEP, DEEP, (7, PLIES + 4, ROWS + 4, SUB, LANE)],
        )
        stress, weights, mobility_rim, *rest = result
        if first:
            free_deep, fixed_deep, *rest = rest
        fields = [stress, warmth, crosslink] + ([fill] if first else [])
        came = exchange(
            par, fields, SECOND[: len(fields)], (True, False, False, False)[: len(fields)], rest
        )
        stress_rim, squares = call(
            residual_kernel,
            [par, stress, weights, mobility_rim, free, *came],
            [RIM, (SUB, LANE)],
            [DEEP, DEEP],
        )
        local_sums.append(jnp.sum(squares))
        outs = [shape] * 3 if last else [BLOCK] * 4 + [(6, ROWS, SUB, LANE)] * 2
        warmth, crosslink, stress, *rest = call(
            functools.partial(transport_kernel, first, last),
            [
                par,
                stress_rim,
                mobility_rim,
                warmth,
                crosslink,
                preform,
                fill if first else fill_rim,
                *came,
            ],
            outs + ([RIM] if first else []),
            [RIM, RIM] + ([line] * 3 if last else []),
        )
        if first:
            fill_rim = rest.pop()
        if not last:
            mobility, *sends = rest
    lane = lax.broadcasted_iota(jnp.int32, (devices, 1, LANE), 2)
    message = jnp.where(lane == 0, local_sums[0], jnp.where(lane == 1, local_sums[1], 0.0))
    parts = lax.all_to_all(message, ("ply", "tile"), 0, 0)
    totals = jnp.sum(parts, axis=(0, 1))[:STEPS]
    imbalance_record = jnp.sqrt(totals / site_total + epsilon)
    return (warmth, crosslink, stress, imbalance_record)


def solution(mesh):
    return jax.shard_map(
        per_device,
        mesh=mesh,
        in_specs=(P("ply", "tile", None),) * 7,
        out_specs=(P("ply", "tile", None), P("ply", "tile", None), P("ply", "tile", None), P()),
        check_vma=False,
    )
```

```python
import functools

import jax
import jax.numpy as jnp
from jax import lax
from jax.experimental import pallas as pl
from jax.experimental.pallas import tpu as pltpu
from jax.sharding import PartitionSpec as P


STEPS = 2


fluidity_barrier = 4.0
fluidity_gelation_coefficient = 2.0
arrhenius_prefactor = 0.2
arrhenius_barrier = 8.0
released_enthalpy = 0.3
diffusion_coefficient = 0.1
clock_step_size = 0.5
epsilon = 1e-06

PLIES, ROWS, SUB, LANE = 4, 8, 8, 128
OFF = 3
DEEP = (PLIES + 2 * OFF, ROWS + 2 * OFF, SUB, LANE)
RIM = (PLIES + 2, ROWS + 2, SUB, LANE)
BLOCK = (PLIES, ROWS, SUB, LANE)


def swap_pairs(count, parity):
    pairs = []
    for i in range(parity, count - 1, 2):
        pairs += [(i, i + 1), (i + 1, i)]
    return pairs


def swap(axis, odd_send, even_send):
    count = lax.axis_size(axis)
    odd = lax.ppermute(odd_send, axis, swap_pairs(count, 1))
    even = lax.ppermute(even_send, axis, swap_pairs(count, 0))
    return odd, even


def cell_index(shape):
    return LANE * lax.broadcasted_iota(jnp.int32, shape, 1) + lax.broadcasted_iota(
        jnp.int32, shape, 2
    )


def next_cell(x):
    moved = pltpu.roll(x, LANE - 1, 2)
    lane = lax.broadcasted_iota(jnp.int32, x.shape, 2)
    return jnp.where(lane == LANE - 1, pltpu.roll(moved, SUB - 1, 1), moved)


def previous_cell(x):
    moved = pltpu.roll(x, 1, 2)
    lane = lax.broadcasted_iota(jnp.int32, x.shape, 2)
    return jnp.where(lane == 0, pltpu.roll(moved, 1, 1), moved)


def beside(ref, i, top, end, walled=False):
    centre = ref[i, top:end]
    after, before = next_cell(centre), previous_cell(centre)
    if walled:
        cell = cell_index(centre.shape)
        after = jnp.where(cell == SUB * LANE - 1, 0.0, after)
        before = jnp.where(cell == 0, 0.0, before)
    return centre, [
        ref[i + 1, top:end],
        ref[i - 1, top:end],
        ref[i, top + 1 : end + 1],
        ref[i, top - 1 : end - 1],
        after,
        before,
    ]


def face_list(mobility, i, top, end):
    centre, around = beside(mobility, i, top, end, walled=True)
    result = []
    for other in around:
        denom = centre + other
        result.append(2.0 * centre * other / jnp.where(denom > 0, denom, 1.0))
    return result


def mobility_of(preform, warmth, crosslink):
    return preform * jnp.exp(
        -(
            fluidity_barrier * (1.0 / warmth - 1.0)
            + fluidity_gelation_coefficient * crosslink
        )
    )


def loop(count, body):
    def step(i, carry):
        body(i)
        return carry

    lax.fori_loop(0, count, step, 0)


def pack_plies(par, local, depth, odd_out, even_out, unit):
    last = PLIES - depth
    odd_out[unit : unit + depth] = local[pl.ds(par[0] * last, depth)]
    even_out[unit : unit + depth] = local[pl.ds((1 - par[0]) * last, depth)]


def pack_rows(par, local, odd_in, even_in, unit, depth, odd_out, even_out, base, corners=True):
    last = ROWS - depth
    for out, start in ((odd_out, par[1] * last), (even_out, (1 - par[1]) * last)):
        skip = depth if corners else 0
        for i in range(PLIES):
            at = base + (skip + i) * depth
            out[at : at + depth] = local[i, pl.ds(start, depth)]
        if corners:
            for came, first in (
                (odd_in, par[0] * (PLIES + depth)),
                (even_in, (1 - par[0]) * (PLIES + depth)),
            ):
                for i in range(depth):
                    out[pl.ds(base + (first + i) * depth, depth)] = came[
                        unit + i, pl.ds(start, depth)
                    ]


def assemble(par, dst, off, local, ply_in, unit, row_in, base, depth, corners=True):
    for i in range(PLIES):
        dst[off + i, off : off + ROWS] = local[i]
    for came, side in zip(ply_in, (par[0], 1 - par[0]), strict=True):
        first = off - depth + side * (PLIES + depth)
        for i in range(depth):
            dst[first + i, off : off + ROWS] = came[unit + i]
    skip = 0 if corners else depth
    for came, side in zip(row_in, (par[1], 1 - par[1]), strict=True):
        first = off - depth + side * (ROWS + depth)
        for i in range(PLIES + 2 * (depth - skip)):
            at = base + i * depth
            dst[off - depth + skip + i, pl.ds(first, depth)] = came[at : at + depth]


def to_lines(flat, lines, i):
    for j in range(SUB):
        part = flat[i, :, j * LANE : (j + 1) * LANE].astype(jnp.float32)
        lines[pl.ds(j, ROWS, stride=SUB), :] = part
    return lines[...].reshape(ROWS, SUB, LANE)


def from_lines(value, lines, flat, i):
    lines[...] = value.reshape(ROWS * SUB, LANE)
    for j in range(SUB):
        flat[i, :, j * LANE : (j + 1) * LANE] = lines[pl.ds(j, ROWS, stride=SUB), :]


def prepare_kernel(
    par, warmth, crosslink, stress, preform, wetted, inlet, outlet,
    warmth_out, crosslink_out, stress_out, preform_out, mobility, free, fixed, fill,
    odd_out, even_out, *lines,
):
    for i in range(PLIES):
        t = to_lines(warmth, lines[0], i)
        c = to_lines(crosslink, lines[1], i)
        k = to_lines(preform, lines[2], i)
        warmth_out[i] = t
        crosslink_out[i] = c
        preform_out[i] = k
        mobility[i] = mobility_of(k, t, c)
        stress_out[i] = to_lines(stress, lines[3], i)
        w = to_lines(wetted, lines[4], i)
        n = to_lines(inlet, lines[5], i)
        o = to_lines(outlet, lines[6], i)
        fill[i] = w
        fixed[i] = n
        free[i] = w * (1.0 - n) * (1.0 - o)
    pack_plies(par, stress_out, 3, odd_out, even_out, 0)
    pack_plies(par, mobility, 3, odd_out, even_out, 3)
    pack_plies(par, free, 2, odd_out, even_out, 6)
    pack_plies(par, fixed, 2, odd_out, even_out, 8)


FIRST = ((0, 0, 3), (3, 30, 3), (6, 60, 2), (8, 76, 2))


def rows_kernel(layout, corners, par, *refs):
    n = len(layout)
    odd_in, even_in, odd_out, even_out = refs[n:]
    for local, (unit, base, depth), corner in zip(refs[:n], layout, corners, strict=True):
        pack_rows(par, local, odd_in, even_in, unit, depth, odd_out, even_out, base, corner)


def sweep(source, target, weights, shift, depth):
    top, end = OFF - depth, OFF + ROWS + depth

    def ply(k):
        i = OFF - depth + k
        _, around = beside(source, i, top, end)
        rows = slice(top - shift, end - shift)
        total = weights[6, i - shift, rows]
        for f in range(6):
            total = total + weights[f, i - shift, rows] * around[f]
        target[i, top:end] = total

    loop(PLIES + 2 * depth, ply)


def sweeps_kernel(first, par, *refs):
    if first:
        (stress, mobility, free, fixed, warmth, crosslink, fill,
         odd_in, even_in, odd_rows, even_rows,
         stress_out, weights_out, mobility_out, free_deep, fixed_deep, odd_out, even_out,
         p0, p1, m, weights) = refs
    else:
        (stress, mobility, free_deep, fixed_deep, warmth, crosslink,
         odd_in, even_in, odd_rows, even_rows,
         stress_out, weights_out, mobility_out, odd_out, even_out,
         p0, p1, m, weights) = refs
    fields = [(p0, stress), (m, mobility)]
    if first:
        fields += [(free_deep, free), (fixed_deep, fixed)]
    for (dst, local), (unit, base, depth) in zip(fields, FIRST, strict=False):
        assemble(par, dst, OFF, local, (odd_in, even_in), unit, (odd_rows, even_rows), base, depth)
    top, end = 1, OFF + ROWS + 2

    def weigh(k):
        i = 1 + k
        faces = face_list(m, i, top, end)
        is_free = free_deep[i, top:end] > 0
        total = faces[0]
        for f in range(1, 6):
            total = total + faces[f]
        scale = jnp.where(is_free, 1.0 / jnp.where(is_free, total, 1.0), 0.0)
        for f in range(6):
            weights[f, k] = faces[f] * scale
        weights[6, k] = jnp.where(is_free, 0.0, fixed_deep[i, top:end])

    loop(PLIES + 4, weigh)
    sweep(p0, p1, weights, 1, 2)
    sweep(p1, p0, weights, 1, 1)
    sweep(p0, p1, weights, 1, 0)
    for i in range(PLIES):
        stress_out[i] = p1[OFF + i, OFF : OFF + ROWS]

    def keep(k):
        mobility_out[k] = m[k + OFF - 1, OFF - 1 : OFF + ROWS + 1]
        for f in range(7):
            weights_out[f, k] = weights[f, k + 1, 1 : 1 + ROWS + 2]

    loop(PLIES + 2, keep)
    pack_plies(par, stress_out, 2, odd_out, even_out, 0)
    pack_plies(par, warmth, 1, odd_out, even_out, 2)
    pack_plies(par, crosslink, 1, odd_out, even_out, 3)
    if first:
        pack_plies(par, fill, 1, odd_out, even_out, 4)


SECOND = ((0, 0, 2), (2, 16, 1), (3, 20, 1), (4, 24, 1))


def residual_kernel(
    par, stress, weights, mobility, free, odd_in, even_in, odd_rows, even_rows,
    stress_rim, squares, p0, p1,
):
    assemble(par, p0, OFF, stress, (odd_in, even_in), 0, (odd_rows, even_rows), 0, 2)
    sweep(p0, p1, weights, OFF - 1, 1)
    squares[...] = jnp.zeros((SUB, LANE), jnp.float32)

    def ply(k):
        centre, around = beside(p1, OFF + k, OFF, OFF + ROWS)
        faces = face_list(mobility, 1 + k, 1, 1 + ROWS)
        weighted = faces[0] * around[0]
        total = faces[0]
        for f in range(1, 6):
            weighted = weighted + faces[f] * around[f]
            total = total + faces[f]
        imbalance = free[k] * (weighted - total * centre)
        squares[...] += jnp.sum(imbalance * imbalance, axis=0)

    loop(PLIES, ply)

    def keep(k):
        stress_rim[k] = p1[k + OFF - 1, OFF - 1 : OFF + ROWS + 1]

    loop(PLIES + 2, keep)


def last_residual_kernel(
    par, stress, weights, mobility, free, odd_in, even_in, odd_rows, even_rows, earlier,
    stress_rim, message, p0, p1, squares,
):
    residual_kernel(
        par, stress, weights, mobility, free, odd_in, even_in, odd_rows, even_rows,
        stress_rim, squares, p0, p1,
    )
    lane = lax.broadcasted_iota(jnp.int32, message.shape, 1)
    message[...] = jnp.where(
        lane == 0,
        jnp.sum(earlier[...]),
        jnp.where(lane == 1, jnp.sum(squares[...]), 0.0),
    )


def step_end_kernel(
    par, stress, weights, mobility, free, warmth, crosslink, preform, fill,
    odd_in, even_in, odd_rows, even_rows,
    warmth_out, crosslink_out, stress_out, mobility_out, odd_out, even_out, fill_rim, squares,
    stress_rim, p0, p1, t_rim, c_rim,
):
    residual_kernel(
        par, stress, weights, mobility, free, odd_in, even_in, odd_rows, even_rows,
        stress_rim, squares, p0, p1,
    )
    transport_kernel(
        True, False, par, stress_rim, mobility, warmth, crosslink, preform, fill,
        odd_in, even_in, odd_rows, even_rows,
        warmth_out, crosslink_out, stress_out, mobility_out, odd_out, even_out, fill_rim,
        t_rim, c_rim,
    )


def transport_kernel(first, last, par, *refs):
    stress_rim, mobility, warmth, crosslink, preform = refs[:5]
    if first:
        fill, refs = refs[5], refs[6:]
    else:
        fill_rim, refs = refs[5], refs[6:]
    odd_in, even_in, odd_rows, even_rows = refs[:4]
    refs = refs[4:]
    if last:
        warmth_out, crosslink_out, stress_out = refs[:3]
        refs = refs[3:]
    else:
        warmth_out, crosslink_out, stress_out, mobility_out, odd_out, even_out = refs[:6]
        refs = refs[6:]
    if first:
        fill_rim, refs = refs[0], refs[1:]
    t_rim, c_rim = refs[:2]
    lines = refs[2:]
    fields = [(t_rim, warmth), (c_rim, crosslink)]
    if first:
        fields.append((fill_rim, fill))
    for (dst, local), (unit, base, depth) in zip(fields, SECOND[1:], strict=False):
        assemble(
            par, dst, 1, local, (odd_in, even_in), unit, (odd_rows, even_rows), base, depth, False
        )

    def ply(k):
        i, top, end = 1 + k, 1, 1 + ROWS
        stress, near_stress = beside(stress_rim, i, top, end)
        t, near_t = beside(t_rim, i, top, end)
        c, near_c = beside(c_rim, i, top, end)
        full, near_full = beside(fill_rim, i, top, end, walled=True)
        faces = face_list(mobility, i, top, end)
        t_gain = jnp.zeros_like(t)
        c_gain = jnp.zeros_like(t)
        spread = jnp.zeros_like(t)
        for f in range(6):
            inward = jnp.maximum(faces[f] * (near_stress[f] - stress), 0.0) * near_full[f]
            t_step = near_t[f] - t
            t_gain = t_gain + inward * t_step
            c_gain = c_gain + inward * (near_c[f] - c)
            spread = spread + near_full[f] * t_step
        speed = (
            arrhenius_prefactor * jnp.exp(arrhenius_barrier * (1.0 - 1.0 / t)) * (1.0 - c)
        )
        t_new = t + full * clock_step_size * (
            t_gain + diffusion_coefficient * spread + released_enthalpy * speed
        )
        c_new = c + full * clock_step_size * (c_gain + speed)
        if last:
            from_lines(t_new, lines[0], warmth_out, k)
            from_lines(c_new, lines[1], crosslink_out, k)
            from_lines(stress, lines[2], stress_out, k)
        else:
            warmth_out[k] = t_new
            crosslink_out[k] = c_new
            stress_out[k] = stress
            mobility_out[k] = mobility_of(preform[k], t_new, c_new)

    if last:
        for k in range(PLIES):
            ply(k)
    else:
        loop(PLIES, ply)
        pack_plies(par, stress_out, 3, odd_out, even_out, 0)
        pack_plies(par, mobility_out, 3, odd_out, even_out, 3)


def call(kernel, args, outs, scratch=()):
    vmem = pl.BlockSpec(memory_space=pltpu.VMEM)
    return pl.pallas_call(
        kernel,
        out_shape=[jax.ShapeDtypeStruct(shape, jnp.float32) for shape in outs],
        in_specs=[pl.BlockSpec(memory_space=pltpu.SMEM)] + [vmem] * (len(args) - 1),
        out_specs=[vmem] * len(outs),
        scratch_shapes=[pltpu.VMEM(shape, jnp.float32) for shape in scratch],
        compiler_params=pltpu.CompilerParams(vmem_limit_bytes=16 << 20),
    )(*args)


def exchange(par, fields, layout, corners, sends):
    came = swap("ply", *sends)
    lines = sum(
        (PLIES + (2 * depth if corner else 0)) * depth
        for (_, _, depth), corner in zip(layout, corners, strict=True)
    )
    rows = call(
        functools.partial(rows_kernel, layout, corners),
        [par, *fields, *came],
        [(lines, SUB, LANE)] * 2,
    )
    return (*came, *swap("tile", *rows))


def per_device(
    scaled_warmth,
    crosslink_fraction,
    fluid_stress,
    preform_porosity_coefficient,
    wetted_flags,
    injection_flags,
    outlet_flags,
):
    devices = lax.axis_size("ply") * lax.axis_size("tile")
    site_total = scaled_warmth.size * devices
    shape = scaled_warmth.shape
    assert shape == (PLIES, ROWS, SUB * LANE)
    pair = lax.broadcasted_iota(jnp.int32, (2,), 0)
    par = jnp.where(pair == 0, lax.axis_index("ply") % 2, lax.axis_index("tile") % 2)
    line = (ROWS * SUB, LANE)
    (warmth, crosslink, stress, preform, mobility, free, fixed, fill, *sends) = call(
        prepare_kernel,
        [
            par,
            scaled_warmth,
            crosslink_fraction,
            fluid_stress,
            preform_porosity_coefficient,
            wetted_flags,
            injection_flags,
            outlet_flags,
        ],
        [BLOCK] * 8 + [(10, ROWS, SUB, LANE)] * 2,
        [line] * 7,
    )
    for repeat in range(STEPS):
        first = repeat == 0
        fields = [stress, mobility] + ([free, fixed] if first else [])
        count = len(fields)
        came = exchange(par, fields, FIRST[:count], (True,) * count, sends)
        units = 5 if first else 4
        args = fields if first else fields + [free_deep, fixed_deep]
        result = call(
            functools.partial(sweeps_kernel, first),
            [par, *args, warmth, crosslink, *([fill] if first else []), *came],
            [BLOCK, (7, *RIM), RIM]
            + ([DEEP] * 2 if first else [])
            + [(units, ROWS, SUB, LANE)] * 2,
            [DEEP, DEEP, DEEP, (7, PLIES + 4, ROWS + 4, SUB, LANE)],
        )
        stress, weights, mobility_rim, *rest = result
        if first:
            free_deep, fixed_deep, *rest = rest
        fields = [stress, warmth, crosslink] + ([fill] if first else [])
        came = exchange(
            par, fields, SECOND[: len(fields)], (True, False, False, False)[: len(fields)], rest
        )
        if first:
            warmth, crosslink, stress, mobility, *sends, fill_rim, squares = call(
                step_end_kernel,
                [
                    par, stress, weights, mobility_rim, free,
                    warmth, crosslink, preform, fill, *came,
                ],
                [BLOCK] * 4 + [(6, ROWS, SUB, LANE)] * 2 + [RIM, (SUB, LANE)],
                [RIM, DEEP, DEEP, RIM, RIM],
            )
    stress_rim, message = call(
        last_residual_kernel,
        [par, stress, weights, mobility_rim, free, *came, squares],
        [RIM, (devices, LANE)],
        [DEEP, DEEP, (SUB, LANE)],
    )
    message = message.reshape(devices, 1, LANE)
    warmth, crosslink, stress = call(
        functools.partial(transport_kernel, False, True),
        [par, stress_rim, mobility_rim, warmth, crosslink, preform, fill_rim, *came],
        [shape] * 3,
        [RIM, RIM] + [line] * 3,
    )
    parts = lax.all_to_all(message, ("ply", "tile"), 0, 0)
    totals = jnp.sum(parts, axis=(0, 1))[:STEPS]
    imbalance_record = jnp.sqrt(totals / site_total + epsilon)
    return (warmth, crosslink, stress, imbalance_record)


def solution(mesh):
    return jax.shard_map(
        per_device,
        mesh=mesh,
        in_specs=(P("ply", "tile", None),) * 7,
        out_specs=(P("ply", "tile", None), P("ply", "tile", None), P("ply", "tile", None), P()),
        check_vma=False,
    )
```

```python
import functools

import jax
import jax.numpy as jnp
from jax import lax
from jax.experimental import pallas as pl
from jax.experimental.pallas import tpu as pltpu
from jax.sharding import PartitionSpec as P


STEPS = 2


fluidity_barrier = 4.0
fluidity_gelation_coefficient = 2.0
arrhenius_prefactor = 0.2
arrhenius_barrier = 8.0
released_enthalpy = 0.3
diffusion_coefficient = 0.1
clock_step_size = 0.5
epsilon = 1e-06

PLIES, ROWS, SUB, LANE = 4, 8, 8, 128
OFF = 3
DEEP = (PLIES + 2 * OFF, ROWS + 2 * OFF, SUB, LANE)
RIM = (PLIES + 2, ROWS + 2, SUB, LANE)
BLOCK = (PLIES, ROWS, SUB, LANE)


def swap_pairs(count, parity):
    pairs = []
    for i in range(parity, count - 1, 2):
        pairs += [(i, i + 1), (i + 1, i)]
    return pairs


def swap(axis, odd_send, even_send):
    count = lax.axis_size(axis)
    odd = lax.ppermute(odd_send, axis, swap_pairs(count, 1))
    even = lax.ppermute(even_send, axis, swap_pairs(count, 0))
    return odd, even


def cell_index(shape):
    return LANE * lax.broadcasted_iota(jnp.int32, shape, 1) + lax.broadcasted_iota(
        jnp.int32, shape, 2
    )


def next_cell(x):
    moved = pltpu.roll(x, LANE - 1, 2)
    lane = lax.broadcasted_iota(jnp.int32, x.shape, 2)
    return jnp.where(lane == LANE - 1, pltpu.roll(moved, SUB - 1, 1), moved)


def previous_cell(x):
    moved = pltpu.roll(x, 1, 2)
    lane = lax.broadcasted_iota(jnp.int32, x.shape, 2)
    return jnp.where(lane == 0, pltpu.roll(moved, 1, 1), moved)


def beside(ref, i, top, end, walled=False):
    centre = ref[i, top:end]
    after, before = next_cell(centre), previous_cell(centre)
    if walled:
        cell = cell_index(centre.shape)
        after = jnp.where(cell == SUB * LANE - 1, 0.0, after)
        before = jnp.where(cell == 0, 0.0, before)
    return centre, [
        ref[i + 1, top:end],
        ref[i - 1, top:end],
        ref[i, top + 1 : end + 1],
        ref[i, top - 1 : end - 1],
        after,
        before,
    ]


def face_list(mobility, i, top, end):
    centre, around = beside(mobility, i, top, end, walled=True)
    result = []
    for other in around:
        denom = centre + other
        result.append(2.0 * centre * other / jnp.where(denom > 0, denom, 1.0))
    return result


def mobility_of(preform, warmth, crosslink):
    return preform * jnp.exp(
        -(
            fluidity_barrier * (1.0 / warmth - 1.0)
            + fluidity_gelation_coefficient * crosslink
        )
    )


def loop(count, body):
    def step(i, carry):
        body(i)
        return carry

    lax.fori_loop(0, count, step, 0)


def pack_plies(par, local, depth, odd_out, even_out, unit):
    last = PLIES - depth
    odd_out[unit : unit + depth] = local[pl.ds(par[0] * last, depth)]
    even_out[unit : unit + depth] = local[pl.ds((1 - par[0]) * last, depth)]


def pack_rows(par, local, odd_in, even_in, part, odd_out, even_out, corners=True):
    unit, base, depth, near = part
    last = ROWS - depth
    for out, start in ((odd_out, par[1] * last), (even_out, (1 - par[1]) * last)):
        skip = depth - near if corners else 0
        for i in range(PLIES + 2 * near):
            at = base + (skip + i) * depth
            out[at : at + depth] = local[i, pl.ds(start + near, depth)]
        if corners:
            for came, side in ((odd_in, par[0]), (even_in, 1 - par[0])):
                first = side * (PLIES + depth + near)
                for i in range(depth - near):
                    out[pl.ds(base + (first + i) * depth, depth)] = came[
                        unit + i, pl.ds(start, depth)
                    ]


def assemble(par, dst, off, local, ply_in, row_in, part, corners=True):
    unit, base, depth, near = part
    for i in range(PLIES + 2 * near):
        dst[off - near + i, off - near : off + ROWS + near] = local[i]
    for came, side in zip(ply_in, (par[0], 1 - par[0]), strict=True):
        first = off - depth + side * (PLIES + depth + near)
        for i in range(depth - near):
            dst[first + i, off : off + ROWS] = came[unit + i]
    skip = 0 if corners else depth
    for came, side in zip(row_in, (par[1], 1 - par[1]), strict=True):
        first = off - depth + side * (ROWS + depth)
        for i in range(PLIES + 2 * (depth - skip)):
            at = base + i * depth
            dst[off - depth + skip + i, pl.ds(first, depth)] = came[at : at + depth]


def to_lines(flat, lines, i):
    for j in range(SUB):
        part = flat[i, :, j * LANE : (j + 1) * LANE].astype(jnp.float32)
        lines[pl.ds(j, ROWS, stride=SUB), :] = part
    return lines[...].reshape(ROWS, SUB, LANE)


def from_lines(value, lines, flat, i):
    lines[...] = value.reshape(ROWS * SUB, LANE)
    for j in range(SUB):
        flat[i, :, j * LANE : (j + 1) * LANE] = lines[pl.ds(j, ROWS, stride=SUB), :]


def prepare_kernel(
    par, warmth, crosslink, stress, preform, wetted, inlet, outlet,
    warmth_out, crosslink_out, stress_out, preform_out, mobility, free, fixed, fill,
    odd_out, even_out, *scratch,
):
    lines, landed, arrived = scratch[:7], scratch[7:14], scratch[14]
    given = (warmth, crosslink, preform, stress, wetted, inlet, outlet)
    copies = [
        pltpu.make_async_copy(source, target, arrived.at[n])
        for n, (source, target) in enumerate(zip(given, landed, strict=True))
    ]
    for copy in copies:
        copy.start()
    for copy in copies:
        copy.wait()
    warmth, crosslink, preform, stress, wetted, inlet, outlet = landed
    for i in range(PLIES):
        t = to_lines(warmth, lines[0], i)
        c = to_lines(crosslink, lines[1], i)
        k = to_lines(preform, lines[2], i)
        warmth_out[i] = t
        crosslink_out[i] = c
        preform_out[i] = k
        mobility[i] = mobility_of(k, t, c)
        stress_out[i] = to_lines(stress, lines[3], i)
        w = to_lines(wetted, lines[4], i)
        n = to_lines(inlet, lines[5], i)
        o = to_lines(outlet, lines[6], i)
        fill[i] = w
        fixed[i] = n
        free[i] = w * (1.0 - n) * (1.0 - o)
    pack_plies(par, stress_out, 3, odd_out, even_out, 0)
    pack_plies(par, mobility, 3, odd_out, even_out, 3)
    pack_plies(par, free, 2, odd_out, even_out, 6)
    pack_plies(par, fixed, 2, odd_out, even_out, 8)


FIRST = ((0, 0, 3, 0), (3, 30, 3, 0), (6, 60, 2, 0), (8, 76, 2, 0))
FIRST_AGAIN = ((0, 0, 3, 1), (2, 30, 3, 0))


def rows_kernel(layout, corners, par, *refs):
    n = len(layout)
    odd_in, even_in, odd_out, even_out = refs[n:]
    for local, part, corner in zip(refs[:n], layout, corners, strict=True):
        pack_rows(par, local, odd_in, even_in, part, odd_out, even_out, corner)


def sweep(source, target, weights, shift, depth):
    top, end = OFF - depth, OFF + ROWS + depth

    def ply(k):
        i = OFF - depth + k
        _, around = beside(source, i, top, end)
        rows = slice(top - shift, end - shift)
        total = weights[6, i - shift, rows]
        for f in range(6):
            total = total + weights[f, i - shift, rows] * around[f]
        target[i, top:end] = total

    loop(PLIES + 2 * depth, ply)


def sweeps_kernel(first, par, *refs):
    if first:
        (stress, mobility, free, fixed, warmth, crosslink, fill,
         odd_in, even_in, odd_rows, even_rows,
         stress_out, weights_out, mobility_out, free_deep, fixed_deep, odd_out, even_out,
         p0, p1, m, weights) = refs
    else:
        (stress, mobility, free_deep, fixed_deep, warmth, crosslink,
         odd_in, even_in, odd_rows, even_rows,
         stress_out, weights_out, mobility_out, odd_out, even_out,
         p0, p1, m, weights) = refs
    fields = [(p0, stress), (m, mobility)]
    if first:
        fields += [(free_deep, free), (fixed_deep, fixed)]
    for (dst, local), part in zip(fields, FIRST if first else FIRST_AGAIN, strict=True):
        assemble(par, dst, OFF, local, (odd_in, even_in), (odd_rows, even_rows), part)
    top, end = 1, OFF + ROWS + 2

    def weigh(k):
        i = 1 + k
        faces = face_list(m, i, top, end)
        is_free = free_deep[i, top:end] > 0
        total = faces[0]
        for f in range(1, 6):
            total = total + faces[f]
        scale = jnp.where(is_free, 1.0 / jnp.where(is_free, total, 1.0), 0.0)
        for f in range(6):
            weights[f, k] = faces[f] * scale
        weights[6, k] = jnp.where(is_free, 0.0, fixed_deep[i, top:end])

    loop(PLIES + 4, weigh)
    sweep(p0, p1, weights, 1, 2)
    sweep(p1, p0, weights, 1, 1)
    sweep(p0, p1, weights, 1, 0)
    for i in range(PLIES):
        stress_out[i] = p1[OFF + i, OFF : OFF + ROWS]

    def keep(k):
        mobility_out[k] = m[k + OFF - 1, OFF - 1 : OFF + ROWS + 1]
        for f in range(7):
            weights_out[f, k] = weights[f, k + 1, 1 : 1 + ROWS + 2]

    loop(PLIES + 2, keep)
    pack_plies(par, stress_out, 2, odd_out, even_out, 0)
    pack_plies(par, warmth, 1, odd_out, even_out, 2)
    pack_plies(par, crosslink, 1, odd_out, even_out, 3)
    if first:
        pack_plies(par, fill, 1, odd_out, even_out, 4)


SECOND = ((0, 0, 2, 0), (2, 16, 1, 0), (3, 20, 1, 0), (4, 24, 1, 0))


def residual_kernel(
    par, stress, weights, mobility, free, odd_in, even_in, odd_rows, even_rows,
    stress_rim, squares, p0, p1,
):
    assemble(par, p0, OFF, stress, (odd_in, even_in), (odd_rows, even_rows), SECOND[0])
    sweep(p0, p1, weights, OFF - 1, 1)
    squares[...] = jnp.zeros((SUB, LANE), jnp.float32)

    def ply(k):
        centre, around = beside(p1, OFF + k, OFF, OFF + ROWS)
        faces = face_list(mobility, 1 + k, 1, 1 + ROWS)
        weighted = faces[0] * around[0]
        total = faces[0]
        for f in range(1, 6):
            weighted = weighted + faces[f] * around[f]
            total = total + faces[f]
        imbalance = free[k] * (weighted - total * centre)
        squares[...] += jnp.sum(imbalance * imbalance, axis=0)

    loop(PLIES, ply)

    def keep(k):
        stress_rim[k] = p1[k + OFF - 1, OFF - 1 : OFF + ROWS + 1]

    loop(PLIES + 2, keep)


def last_residual_kernel(
    par, stress, weights, mobility, free, odd_in, even_in, odd_rows, even_rows, earlier,
    stress_rim, message, p0, p1, squares,
):
    residual_kernel(
        par, stress, weights, mobility, free, odd_in, even_in, odd_rows, even_rows,
        stress_rim, squares, p0, p1,
    )
    lane = lax.broadcasted_iota(jnp.int32, message.shape, 1)
    message[...] = jnp.where(
        lane == 0,
        jnp.sum(earlier[...]),
        jnp.where(lane == 1, jnp.sum(squares[...]), 0.0),
    )


def step_end_kernel(
    par, stress, weights, mobility, free, warmth, crosslink, preform, fill,
    odd_in, even_in, odd_rows, even_rows,
    warmth_out, crosslink_out, mobility_out, odd_out, even_out, fill_rim, squares, stress_rim,
    p0, p1, t_rim, c_rim,
):
    residual_kernel(
        par, stress, weights, mobility, free, odd_in, even_in, odd_rows, even_rows,
        stress_rim, squares, p0, p1,
    )
    transport_kernel(
        True, False, par, stress_rim, mobility, warmth, crosslink, preform, fill,
        odd_in, even_in, odd_rows, even_rows,
        warmth_out, crosslink_out, mobility_out, odd_out, even_out, fill_rim, t_rim, c_rim,
    )


def transport_kernel(first, last, par, *refs):
    stress_rim, mobility, warmth, crosslink, preform = refs[:5]
    if first:
        fill, refs = refs[5], refs[6:]
    else:
        fill_rim, refs = refs[5], refs[6:]
    odd_in, even_in, odd_rows, even_rows = refs[:4]
    refs = refs[4:]
    if last:
        warmth_out, crosslink_out, stress_out = refs[:3]
        refs = refs[3:]
    else:
        warmth_out, crosslink_out, mobility_out, odd_out, even_out = refs[:5]
        refs = refs[5:]
    if first:
        fill_rim, refs = refs[0], refs[1:]
    t_rim, c_rim = refs[:2]
    lines = refs[2:]
    fields = [(t_rim, warmth), (c_rim, crosslink)]
    if first:
        fields.append((fill_rim, fill))
    for (dst, local), part in zip(fields, SECOND[1:], strict=False):
        assemble(par, dst, 1, local, (odd_in, even_in), (odd_rows, even_rows), part, False)

    def ply(k):
        i, top, end = 1 + k, 1, 1 + ROWS
        stress, near_stress = beside(stress_rim, i, top, end)
        t, near_t = beside(t_rim, i, top, end)
        c, near_c = beside(c_rim, i, top, end)
        full, near_full = beside(fill_rim, i, top, end, walled=True)
        faces = face_list(mobility, i, top, end)
        t_gain = jnp.zeros_like(t)
        c_gain = jnp.zeros_like(t)
        spread = jnp.zeros_like(t)
        for f in range(6):
            inward = jnp.maximum(faces[f] * (near_stress[f] - stress), 0.0) * near_full[f]
            t_step = near_t[f] - t
            t_gain = t_gain + inward * t_step
            c_gain = c_gain + inward * (near_c[f] - c)
            spread = spread + near_full[f] * t_step
        speed = (
            arrhenius_prefactor * jnp.exp(arrhenius_barrier * (1.0 - 1.0 / t)) * (1.0 - c)
        )
        t_new = t + full * clock_step_size * (
            t_gain + diffusion_coefficient * spread + released_enthalpy * speed
        )
        c_new = c + full * clock_step_size * (c_gain + speed)
        if last:
            from_lines(t_new, lines[0], warmth_out, k)
            from_lines(c_new, lines[1], crosslink_out, k)
            from_lines(stress, lines[2], stress_out, k)
        else:
            warmth_out[k] = t_new
            crosslink_out[k] = c_new
            mobility_out[k] = mobility_of(preform[k], t_new, c_new)

    if last:
        for k in range(PLIES):
            ply(k)
    else:
        loop(PLIES, ply)
        for out in (odd_out, even_out):
            out[0:2] = stress_rim[2:4, 1 : 1 + ROWS]
        pack_plies(par, mobility_out, 3, odd_out, even_out, 2)


def call(kernel, args, outs, scratch=(), given=pltpu.VMEM, extra=()):
    vmem = pl.BlockSpec(memory_space=pltpu.VMEM)
    return pl.pallas_call(
        kernel,
        out_shape=[jax.ShapeDtypeStruct(shape, jnp.float32) for shape in outs],
        in_specs=[pl.BlockSpec(memory_space=pltpu.SMEM)]
        + [pl.BlockSpec(memory_space=given)] * (len(args) - 1),
        out_specs=[vmem] * len(outs),
        scratch_shapes=[pltpu.VMEM(shape, jnp.float32) for shape in scratch] + list(extra),
        compiler_params=pltpu.CompilerParams(vmem_limit_bytes=16 << 20),
    )(*args)


def exchange(par, fields, layout, corners, sends):
    came = swap("ply", *sends)
    lines = sum(
        (PLIES + (2 * depth if corner else 0)) * depth
        for (_, _, depth, _), corner in zip(layout, corners, strict=True)
    )
    rows = call(
        functools.partial(rows_kernel, layout, corners),
        [par, *fields, *came],
        [(lines, SUB, LANE)] * 2,
    )
    return (*came, *swap("tile", *rows))


def per_device(
    scaled_warmth,
    crosslink_fraction,
    fluid_stress,
    preform_porosity_coefficient,
    wetted_flags,
    injection_flags,
    outlet_flags,
):
    devices = lax.axis_size("ply") * lax.axis_size("tile")
    site_total = scaled_warmth.size * devices
    shape = scaled_warmth.shape
    assert shape == (PLIES, ROWS, SUB * LANE)
    pair = lax.broadcasted_iota(jnp.int32, (2,), 0)
    par = jnp.where(pair == 0, lax.axis_index("ply") % 2, lax.axis_index("tile") % 2)
    line = (ROWS * SUB, LANE)
    (warmth, crosslink, stress, preform, mobility, free, fixed, fill, *sends) = call(
        prepare_kernel,
        [
            par,
            *(
                pltpu.with_memory_space_constraint(array, pltpu.HBM)
                for array in (
                    scaled_warmth,
                    crosslink_fraction,
                    fluid_stress,
                    preform_porosity_coefficient,
                    wetted_flags,
                    injection_flags,
                    outlet_flags,
                )
            ),
        ],
        [BLOCK] * 8 + [(10, ROWS, SUB, LANE)] * 2,
        [line] * 7 + [shape] * 4,
        pltpu.HBM,
        [pltpu.VMEM(shape, jnp.int32)] * 3 + [pltpu.SemaphoreType.DMA((7,))],
    )
    for repeat in range(STEPS):
        first = repeat == 0
        fields = [stress, mobility] + ([free, fixed] if first else [])
        count = len(fields)
        layout = FIRST if first else FIRST_AGAIN
        came = exchange(par, fields, layout, (True,) * count, sends)
        units = 5 if first else 4
        args = fields if first else fields + [free_deep, fixed_deep]
        result = call(
            functools.partial(sweeps_kernel, first),
            [par, *args, warmth, crosslink, *([fill] if first else []), *came],
            [BLOCK, (7, *RIM), RIM]
            + ([DEEP] * 2 if first else [])
            + [(units, ROWS, SUB, LANE)] * 2,
            [DEEP, DEEP, DEEP, (7, PLIES + 4, ROWS + 4, SUB, LANE)],
        )
        stress, weights, mobility_rim, *rest = result
        if first:
            free_deep, fixed_deep, *rest = rest
        fields = [stress, warmth, crosslink] + ([fill] if first else [])
        came = exchange(
            par, fields, SECOND[: len(fields)], (True, False, False, False)[: len(fields)], rest
        )
        if first:
            warmth, crosslink, mobility, *sends, fill_rim, squares, stress = call(
                step_end_kernel,
                [
                    par, stress, weights, mobility_rim, free,
                    warmth, crosslink, preform, fill, *came,
                ],
                [BLOCK] * 3 + [(5, ROWS, SUB, LANE)] * 2 + [RIM, (SUB, LANE), RIM],
                [DEEP, DEEP, RIM, RIM],
            )
    stress_rim, message = call(
        last_residual_kernel,
        [par, stress, weights, mobility_rim, free, *came, squares],
        [RIM, (devices, LANE)],
        [DEEP, DEEP, (SUB, LANE)],
    )
    message = message.reshape(devices, 1, LANE)
    warmth, crosslink, stress = call(
        functools.partial(transport_kernel, False, True),
        [par, stress_rim, mobility_rim, warmth, crosslink, preform, fill_rim, *came],
        [shape] * 3,
        [RIM, RIM] + [line] * 3,
    )
    parts = lax.all_to_all(message, ("ply", "tile"), 0, 0)
    totals = jnp.sum(parts, axis=(0, 1))[:STEPS]
    imbalance_record = jnp.sqrt(totals / site_total + epsilon)
    return (warmth, crosslink, stress, imbalance_record)


def solution(mesh):
    return jax.shard_map(
        per_device,
        mesh=mesh,
        in_specs=(P("ply", "tile", None),) * 7,
        out_specs=(P("ply", "tile", None), P("ply", "tile", None), P("ply", "tile", None), P()),
        check_vma=False,
    )
```

```python
import functools

import jax
import jax.numpy as jnp
from jax import lax
from jax.experimental import pallas as pl
from jax.experimental.pallas import tpu as pltpu
from jax.sharding import PartitionSpec as P


STEPS = 2


fluidity_barrier = 4.0
fluidity_gelation_coefficient = 2.0
arrhenius_prefactor = 0.2
arrhenius_barrier = 8.0
released_enthalpy = 0.3
diffusion_coefficient = 0.1
clock_step_size = 0.5
epsilon = 1e-06

PLIES, ROWS, SUB, LANE = 4, 8, 8, 128
OFF = 3
DEEP = (PLIES + 2 * OFF, ROWS + 2 * OFF, SUB, LANE)
RIM = (PLIES + 2, ROWS + 2, SUB, LANE)
BLOCK = (PLIES, ROWS, SUB, LANE)


def swap_pairs(count, parity):
    pairs = []
    for i in range(parity, count - 1, 2):
        pairs += [(i, i + 1), (i + 1, i)]
    return pairs


def swap(axis, odd_send, even_send):
    count = lax.axis_size(axis)
    odd = lax.ppermute(odd_send, axis, swap_pairs(count, 1))
    even = lax.ppermute(even_send, axis, swap_pairs(count, 0))
    return odd, even


def cell_index(shape):
    return LANE * lax.broadcasted_iota(jnp.int32, shape, 1) + lax.broadcasted_iota(
        jnp.int32, shape, 2
    )


def next_cell(x):
    moved = pltpu.roll(x, LANE - 1, 2)
    lane = lax.broadcasted_iota(jnp.int32, x.shape, 2)
    return jnp.where(lane == LANE - 1, pltpu.roll(moved, SUB - 1, 1), moved)


def previous_cell(x):
    moved = pltpu.roll(x, 1, 2)
    lane = lax.broadcasted_iota(jnp.int32, x.shape, 2)
    return jnp.where(lane == 0, pltpu.roll(moved, 1, 1), moved)


def beside(ref, i, top, end, walled=False):
    centre = ref[i, top:end]
    after, before = next_cell(centre), previous_cell(centre)
    if walled:
        cell = cell_index(centre.shape)
        after = jnp.where(cell == SUB * LANE - 1, 0.0, after)
        before = jnp.where(cell == 0, 0.0, before)
    return centre, [
        ref[i + 1, top:end],
        ref[i - 1, top:end],
        ref[i, top + 1 : end + 1],
        ref[i, top - 1 : end - 1],
        after,
        before,
    ]


def face_list(mobility, i, top, end):
    centre, around = beside(mobility, i, top, end, walled=True)
    result = []
    for other in around:
        denom = centre + other
        result.append(2.0 * centre * other / jnp.where(denom > 0, denom, 1.0))
    return result


def mobility_of(preform, warmth, crosslink):
    return preform * jnp.exp(
        -(
            fluidity_barrier * (1.0 / warmth - 1.0)
            + fluidity_gelation_coefficient * crosslink
        )
    )


def loop(count, body):
    def step(i, carry):
        body(i)
        return carry

    lax.fori_loop(0, count, step, 0, unroll=True)


def pack_plies(par, local, depth, odd_out, even_out, unit):
    last = PLIES - depth
    odd_out[unit : unit + depth] = local[pl.ds(par[0] * last, depth)]
    even_out[unit : unit + depth] = local[pl.ds((1 - par[0]) * last, depth)]


def pack_rows(par, local, odd_in, even_in, part, odd_out, even_out, corners=True):
    unit, base, depth, near = part
    last = ROWS - depth
    for out, start in ((odd_out, par[1] * last), (even_out, (1 - par[1]) * last)):
        skip = depth - near if corners else 0
        for i in range(PLIES + 2 * near):
            at = base + (skip + i) * depth
            out[at : at + depth] = local[i, pl.ds(start + near, depth)]
        if corners:
            for came, side in ((odd_in, par[0]), (even_in, 1 - par[0])):
                first = side * (PLIES + depth + near)
                for i in range(depth - near):
                    out[pl.ds(base + (first + i) * depth, depth)] = came[
                        unit + i, pl.ds(start, depth)
                    ]


def assemble(par, dst, off, local, ply_in, row_in, part, corners=True):
    unit, base, depth, near = part
    for i in range(PLIES + 2 * near):
        dst[off - near + i, off - near : off + ROWS + near] = local[i]
    for came, side in zip(ply_in, (par[0], 1 - par[0]), strict=True):
        first = off - depth + side * (PLIES + depth + near)
        for i in range(depth - near):
            dst[first + i, off : off + ROWS] = came[unit + i]
    skip = 0 if corners else depth
    for came, side in zip(row_in, (par[1], 1 - par[1]), strict=True):
        first = off - depth + side * (ROWS + depth)
        for i in range(PLIES + 2 * (depth - skip)):
            at = base + i * depth
            dst[off - depth + skip + i, pl.ds(first, depth)] = came[at : at + depth]


def to_lines(flat, lines, i):
    for j in range(SUB):
        part = flat[i, :, j * LANE : (j + 1) * LANE].astype(jnp.float32)
        lines[pl.ds(j, ROWS, stride=SUB), :] = part
    return lines[...].reshape(ROWS, SUB, LANE)


def from_lines(value, lines, flat, i):
    lines[...] = value.reshape(ROWS * SUB, LANE)
    for j in range(SUB):
        flat[i, :, j * LANE : (j + 1) * LANE] = lines[pl.ds(j, ROWS, stride=SUB), :]


def prepare_kernel(
    par, warmth, crosslink, stress, preform, wetted, inlet, outlet,
    warmth_out, crosslink_out, stress_out, preform_out, mobility, free, fixed, fill,
    odd_out, even_out, *scratch,
):
    lines, landed, arrived = scratch[:7], scratch[7:14], scratch[14]
    given = (warmth, crosslink, preform, stress, wetted, inlet, outlet)
    copies = [
        pltpu.make_async_copy(source, target, arrived.at[n])
        for n, (source, target) in enumerate(zip(given, landed, strict=True))
    ]
    for copy in copies:
        copy.start()
    for copy in copies:
        copy.wait()
    warmth, crosslink, preform, stress, wetted, inlet, outlet = landed
    for i in range(PLIES):
        t = to_lines(warmth, lines[0], i)
        c = to_lines(crosslink, lines[1], i)
        k = to_lines(preform, lines[2], i)
        warmth_out[i] = t
        crosslink_out[i] = c
        preform_out[i] = k
        mobility[i] = mobility_of(k, t, c)
        stress_out[i] = to_lines(stress, lines[3], i)
        w = to_lines(wetted, lines[4], i)
        n = to_lines(inlet, lines[5], i)
        o = to_lines(outlet, lines[6], i)
        fill[i] = w
        fixed[i] = n
        free[i] = w * (1.0 - n) * (1.0 - o)
    pack_plies(par, stress_out, 2, odd_out, even_out, 0)
    pack_plies(par, mobility, 3, odd_out, even_out, 2)
    pack_plies(par, free, 2, odd_out, even_out, 5)
    pack_plies(par, fixed, 1, odd_out, even_out, 7)


FIRST = ((0, 0, 2, 0), (2, 16, 3, 0), (5, 46, 2, 0), (7, 62, 1, 0))
FIRST_AGAIN = ((0, 0, 2, 1), (1, 16, 3, 0))


def rows_kernel(layout, corners, par, *refs):
    n = len(layout)
    odd_in, even_in, odd_out, even_out = refs[n:]
    for local, part, corner in zip(refs[:n], layout, corners, strict=True):
        pack_rows(par, local, odd_in, even_in, part, odd_out, even_out, corner)


def sweep(source, target, weights, depth, held=None):
    top, end = OFF - depth, OFF + ROWS + depth

    def ply(k):
        i = OFF - depth + k
        centre, around = beside(source, i, top, end)
        rows = slice(top - 1, end - 1)
        total = weights[6, i - 1, rows] * (centre if held is None else held[i, top:end])
        for f in range(6):
            total = total + weights[f, i - 1, rows] * around[f]
        target[i, top:end] = total

    loop(PLIES + 2 * depth, ply)


def sweeps_kernel(first, par, *refs):
    if first:
        (stress, mobility, free, fixed, warmth, crosslink, fill,
         odd_in, even_in, odd_rows, even_rows,
         stress_out, weights, mobility_out, free_deep, odd_out, even_out,
         p0, p1, m, fixed_deep) = refs
        fields = [(p0, stress), (m, mobility), (free_deep, free), (fixed_deep, fixed)]
    else:
        (stress, mobility, free_deep, warmth, crosslink,
         odd_in, even_in, odd_rows, even_rows,
         stress_out, weights, mobility_out, odd_out, even_out,
         p0, p1, m) = refs
        fields = [(p0, stress), (m, mobility)]
        fixed_deep = None
    for (dst, local), part in zip(fields, FIRST if first else FIRST_AGAIN, strict=True):
        assemble(par, dst, OFF, local, (odd_in, even_in), (odd_rows, even_rows), part)
    top, end = 1, OFF + ROWS + 2

    def weigh(k):
        i = 1 + k
        faces = face_list(m, i, top, end)
        is_free = free_deep[i, top:end] > 0
        total = faces[0]
        for f in range(1, 6):
            total = total + faces[f]
        scale = jnp.where(is_free, 1.0 / jnp.where(is_free, total, 1.0), 0.0)
        for f in range(6):
            weights[f, k] = faces[f] * scale
        weights[6, k] = jnp.where(is_free, 0.0, 1.0)

    loop(PLIES + 4, weigh)
    sweep(p0, p1, weights, 1, fixed_deep)
    sweep(p1, p0, weights, 0)
    for i in range(PLIES):
        stress_out[i] = p0[OFF + i, OFF : OFF + ROWS]

    def keep(k):
        mobility_out[k] = m[k + OFF - 1, OFF - 1 : OFF + ROWS + 1]

    loop(PLIES + 2, keep)
    pack_plies(par, stress_out, 3, odd_out, even_out, 0)
    pack_plies(par, warmth, 1, odd_out, even_out, 3)
    pack_plies(par, crosslink, 1, odd_out, even_out, 4)
    if first:
        pack_plies(par, fill, 1, odd_out, even_out, 5)


SECOND = ((0, 0, 3, 0), (3, 30, 1, 0), (4, 34, 1, 0), (5, 38, 1, 0))


def residual_kernel(
    par, stress, weights, mobility, free, odd_in, even_in, odd_rows, even_rows,
    stress_rim, squares, p0, p1,
):
    assemble(par, p0, OFF, stress, (odd_in, even_in), (odd_rows, even_rows), SECOND[0])
    sweep(p0, p1, weights, 2)
    sweep(p1, p0, weights, 1)
    squares[...] = jnp.zeros((SUB, LANE), jnp.float32)

    def ply(k):
        centre, around = beside(p0, OFF + k, OFF, OFF + ROWS)
        faces = face_list(mobility, 1 + k, 1, 1 + ROWS)
        weighted = faces[0] * around[0]
        total = faces[0]
        for f in range(1, 6):
            weighted = weighted + faces[f] * around[f]
            total = total + faces[f]
        imbalance = free[k] * (weighted - total * centre)
        squares[...] += jnp.sum(imbalance * imbalance, axis=0)

    loop(PLIES, ply)

    def keep(k):
        stress_rim[k] = p0[k + OFF - 1, OFF - 1 : OFF + ROWS + 1]

    loop(PLIES + 2, keep)


def last_residual_kernel(
    par, stress, weights, mobility, free, odd_in, even_in, odd_rows, even_rows, earlier,
    stress_rim, message, p0, p1, squares,
):
    residual_kernel(
        par, stress, weights, mobility, free, odd_in, even_in, odd_rows, even_rows,
        stress_rim, squares, p0, p1,
    )
    lane = lax.broadcasted_iota(jnp.int32, message.shape, 1)
    message[...] = jnp.where(
        lane == 0,
        jnp.sum(earlier[...]),
        jnp.where(lane == 1, jnp.sum(squares[...]), 0.0),
    )


def step_end_kernel(
    par, stress, weights, mobility, free, warmth, crosslink, preform, fill,
    odd_in, even_in, odd_rows, even_rows,
    warmth_out, crosslink_out, mobility_out, odd_out, even_out, fill_rim, squares, stress_rim,
    p0, p1, t_rim, c_rim,
):
    residual_kernel(
        par, stress, weights, mobility, free, odd_in, even_in, odd_rows, even_rows,
        stress_rim, squares, p0, p1,
    )
    transport_kernel(
        True, False, par, stress_rim, mobility, warmth, crosslink, preform, fill,
        odd_in, even_in, odd_rows, even_rows,
        warmth_out, crosslink_out, mobility_out, odd_out, even_out, fill_rim, t_rim, c_rim,
    )


def transport_kernel(first, last, par, *refs):
    stress_rim, mobility, warmth, crosslink, preform = refs[:5]
    if first:
        fill, refs = refs[5], refs[6:]
    else:
        fill_rim, refs = refs[5], refs[6:]
    odd_in, even_in, odd_rows, even_rows = refs[:4]
    refs = refs[4:]
    if last:
        warmth_out, crosslink_out, stress_out = refs[:3]
        refs = refs[3:]
    else:
        warmth_out, crosslink_out, mobility_out, odd_out, even_out = refs[:5]
        refs = refs[5:]
    if first:
        fill_rim, refs = refs[0], refs[1:]
    t_rim, c_rim = refs[:2]
    lines = refs[2:]
    fields = [(t_rim, warmth), (c_rim, crosslink)]
    if first:
        fields.append((fill_rim, fill))
    for (dst, local), part in zip(fields, SECOND[1:], strict=False):
        assemble(par, dst, 1, local, (odd_in, even_in), (odd_rows, even_rows), part, False)

    def ply(k):
        i, top, end = 1 + k, 1, 1 + ROWS
        stress, near_stress = beside(stress_rim, i, top, end)
        t, near_t = beside(t_rim, i, top, end)
        c, near_c = beside(c_rim, i, top, end)
        full, near_full = beside(fill_rim, i, top, end, walled=True)
        faces = face_list(mobility, i, top, end)
        t_gain = jnp.zeros_like(t)
        c_gain = jnp.zeros_like(t)
        spread = jnp.zeros_like(t)
        for f in range(6):
            inward = jnp.maximum(faces[f] * (near_stress[f] - stress), 0.0) * near_full[f]
            t_step = near_t[f] - t
            t_gain = t_gain + inward * t_step
            c_gain = c_gain + inward * (near_c[f] - c)
            spread = spread + near_full[f] * t_step
        speed = (
            arrhenius_prefactor * jnp.exp(arrhenius_barrier * (1.0 - 1.0 / t)) * (1.0 - c)
        )
        t_new = t + full * clock_step_size * (
            t_gain + diffusion_coefficient * spread + released_enthalpy * speed
        )
        c_new = c + full * clock_step_size * (c_gain + speed)
        if last:
            from_lines(t_new, lines[0], warmth_out, k)
            from_lines(c_new, lines[1], crosslink_out, k)
            from_lines(stress, lines[2], stress_out, k)
        else:
            warmth_out[k] = t_new
            crosslink_out[k] = c_new
            mobility_out[k] = mobility_of(preform[k], t_new, c_new)

    if last:
        for k in range(PLIES):
            ply(k)
    else:
        loop(PLIES, ply)
        odd_out[0] = stress_rim[2 + par[0], 1 : 1 + ROWS]
        even_out[0] = stress_rim[3 - par[0], 1 : 1 + ROWS]
        pack_plies(par, mobility_out, 3, odd_out, even_out, 1)


def call(kernel, args, outs, scratch=(), given=pltpu.VMEM, extra=()):
    vmem = pl.BlockSpec(memory_space=pltpu.VMEM)
    return pl.pallas_call(
        kernel,
        out_shape=[jax.ShapeDtypeStruct(shape, jnp.float32) for shape in outs],
        in_specs=[pl.BlockSpec(memory_space=pltpu.SMEM)]
        + [pl.BlockSpec(memory_space=given)] * (len(args) - 1),
        out_specs=[vmem] * len(outs),
        scratch_shapes=[pltpu.VMEM(shape, jnp.float32) for shape in scratch] + list(extra),
        compiler_params=pltpu.CompilerParams(vmem_limit_bytes=16 << 20),
    )(*args)


def exchange(par, fields, layout, corners, sends):
    came = swap("ply", *sends)
    lines = sum(
        (PLIES + (2 * depth if corner else 0)) * depth
        for (_, _, depth, _), corner in zip(layout, corners, strict=True)
    )
    rows = call(
        functools.partial(rows_kernel, layout, corners),
        [par, *fields, *came],
        [(lines, SUB, LANE)] * 2,
    )
    return (*came, *swap("tile", *rows))


def per_device(
    scaled_warmth,
    crosslink_fraction,
    fluid_stress,
    preform_porosity_coefficient,
    wetted_flags,
    injection_flags,
    outlet_flags,
):
    devices = lax.axis_size("ply") * lax.axis_size("tile")
    site_total = scaled_warmth.size * devices
    shape = scaled_warmth.shape
    assert shape == (PLIES, ROWS, SUB * LANE)
    pair = lax.broadcasted_iota(jnp.int32, (2,), 0)
    par = jnp.where(pair == 0, lax.axis_index("ply") % 2, lax.axis_index("tile") % 2)
    line = (ROWS * SUB, LANE)
    (warmth, crosslink, stress, preform, mobility, free, fixed, fill, *sends) = call(
        prepare_kernel,
        [
            par,
            *(
                pltpu.with_memory_space_constraint(array, pltpu.HBM)
                for array in (
                    scaled_warmth,
                    crosslink_fraction,
                    fluid_stress,
                    preform_porosity_coefficient,
                    wetted_flags,
                    injection_flags,
                    outlet_flags,
                )
            ),
        ],
        [BLOCK] * 8 + [(8, ROWS, SUB, LANE)] * 2,
        [line] * 7 + [shape] * 4,
        pltpu.HBM,
        [pltpu.VMEM(shape, jnp.int32)] * 3 + [pltpu.SemaphoreType.DMA((7,))],
    )
    for repeat in range(STEPS):
        first = repeat == 0
        fields = [stress, mobility] + ([free, fixed] if first else [])
        count = len(fields)
        layout = FIRST if first else FIRST_AGAIN
        came = exchange(par, fields, layout, (True,) * count, sends)
        units = 6 if first else 5
        args = fields if first else fields + [free_deep]
        result = call(
            functools.partial(sweeps_kernel, first),
            [par, *args, warmth, crosslink, *([fill] if first else []), *came],
            [BLOCK, (7, PLIES + 4, ROWS + 4, SUB, LANE), RIM]
            + ([DEEP] if first else [])
            + [(units, ROWS, SUB, LANE)] * 2,
            [DEEP] * (4 if first else 3),
        )
        stress, weights, mobility_rim, *rest = result
        if first:
            free_deep, *rest = rest
        fields = [stress, warmth, crosslink] + ([fill] if first else [])
        came = exchange(
            par, fields, SECOND[: len(fields)], (True, False, False, False)[: len(fields)], rest
        )
        if first:
            warmth, crosslink, mobility, *sends, fill_rim, squares, stress = call(
                step_end_kernel,
                [
                    par, stress, weights, mobility_rim, free,
                    warmth, crosslink, preform, fill, *came,
                ],
                [BLOCK] * 3 + [(4, ROWS, SUB, LANE)] * 2 + [RIM, (SUB, LANE), RIM],
                [DEEP, DEEP, RIM, RIM],
            )
    stress_rim, message = call(
        last_residual_kernel,
        [par, stress, weights, mobility_rim, free, *came, squares],
        [RIM, (devices, LANE)],
        [DEEP, DEEP, (SUB, LANE)],
    )
    message = message.reshape(devices, 1, LANE)
    warmth, crosslink, stress = call(
        functools.partial(transport_kernel, False, True),
        [par, stress_rim, mobility_rim, warmth, crosslink, preform, fill_rim, *came],
        [shape] * 3,
        [RIM, RIM] + [line] * 3,
    )
    parts = lax.all_to_all(message, ("ply", "tile"), 0, 0)
    totals = jnp.sum(parts, axis=(0, 1))[:STEPS]
    imbalance_record = jnp.sqrt(totals / site_total + epsilon)
    return (warmth, crosslink, stress, imbalance_record)


def solution(mesh):
    return jax.shard_map(
        per_device,
        mesh=mesh,
        in_specs=(P("ply", "tile", None),) * 7,
        out_specs=(P("ply", "tile", None), P("ply", "tile", None), P("ply", "tile", None), P()),
        check_vma=False,
    )
```
